128 devices in a mesh: ctx: 16 (over y_hi, x, core), head: 8 (over y_lo, z).
Axes of the slice: x: 4, y: 4 (y_hi: 2, y_lo: 2; y = y_hi * 2 + y_lo), z: 4, core: 2. Of those that a mesh axis runs over, the one named last changes fastest.
Arguments:
- block_order: int32 [32], replicated, may hold values from 0 to 31, each once
- queries: bfloat16 [3584, 64, 576], P('ctx', 'head'), may hold values from -10 to 10
- keys: bfloat16 [3584, 576], P('ctx'), may hold values from -4 to 4
- dout: bfloat16 [3584, 64, 512], P('ctx', 'head'), may hold values from -6 to 6
Outputs:
- grad_queries: bfloat16 [3584, 64, 576], P('ctx', 'head')
- grad_keys: float32 [3584, 576], P('ctx')
The draws below stay inside these ranges and needn't reach their ends.
Inputs may be any that keep to these rules, and one draw needn't show every extreme that they name: block_order holds each of 0 to 31 once.
All inputs are finite; a program needn't handle non-finite values.
Results may differ from the reference program's by a relative error of at most 0.0048.
Values may be sent and summed in bfloat16 or wider, within the bound.
A program may use at most 64 MiB of HBM per device.

```python
import jax
import jax.numpy as jnp
from jax import lax

LAT = 512
ROPE = 64
KDIM = 576
HEADS = 64
SEQ = 3584
BLOCKS = 32


def paired_arrays(key):
    first = jax.random.fold_in(key, 101)
    second = jax.random.fold_in(key, 202)
    third = jax.random.fold_in(key, 303)
    fourth = jax.random.fold_in(key, 404)
    latent = jax.random.truncated_normal(first, -4.0, 4.0, (SEQ, LAT), jnp.float32)
    rotary = jax.random.truncated_normal(second, -4.0, 4.0, (SEQ, ROPE), jnp.float32)
    query_latent = 0.5 * jax.random.truncated_normal(third, -4.0, 4.0, (SEQ, HEADS, LAT), jnp.float32)
    query_rotary = jax.random.truncated_normal(fourth, -4.0, 4.0, (SEQ, HEADS, ROPE), jnp.float32)
    key_array = jnp.concatenate([latent, rotary], axis=1)
    query_array = jnp.concatenate([query_latent, query_rotary], axis=2)
    return (key_array, query_array)


def draw_keys(key, part):
    key_array, query_array = paired_arrays(key)
    return key_array.astype(jnp.bfloat16)


def draw_queries(key, part):
    key_array, query_array = paired_arrays(key)
    return query_array.astype(jnp.bfloat16)


def levels(key, extent, split, smallest, high):
    def one(position, shards_of):
        heights = jax.random.uniform(jax.random.fold_in(jax.random.fold_in(key, 6), position), (shards_of,), jnp.float32, smallest / len(split), high / len(split))
        return jnp.repeat(jnp.exp(heights), extent[position] // shards_of).reshape((-1,) + (1,) * (len(extent) - position - 1))

    factor_of = one(*split[0])
    for cut in split[1:]:
        factor_of = factor_of * one(*cut)
    return factor_of


def noise(own_key, shape, spread, limit, pieces=(), kind=jnp.bfloat16):
    loudness = levels(own_key, shape, pieces, -0.22, 0.18) if pieces else 1.0
    drawn = jax.random.normal(own_key, shape, jnp.float32) * spread * loudness
    return jnp.minimum(jnp.maximum(drawn, -limit), limit).astype(kind)


def setup_inputs(seed: int = 0) -> dict:
    splits = jax.random.split(jax.random.key(seed), 5)
    block_order = jax.random.permutation(splits[0], BLOCKS).astype(jnp.int32)
    queries = draw_queries(jax.random.fold_in(splits[4], 71), 0)
    keys = draw_keys(jax.random.fold_in(splits[4], 71), 0)
    dout = noise(splits[3], (SEQ, HEADS, LAT), 1.0, 6.0, ((0, 16), (1, 8)))
    return {"block_order": block_order, "queries": queries, "keys": keys, "dout": dout}


softmax_scale = 0.1352
masked_value = -1e30


def reference(block_order, queries, keys, dout):
    block_rows = SEQ // BLOCKS
    offsets = jnp.arange(block_rows, dtype=jnp.int32)
    positions = (block_order[:, None].astype(jnp.int32) * block_rows + offsets[None, :]).reshape(SEQ)
    visible = positions[None, :] <= positions[:, None]
    latent_keys = keys[:, :LAT]

    def per_head(total, head_items):
        query, grad_out = head_items
        scores = jnp.dot(query, keys.T, preferred_element_type=jnp.float32) * softmax_scale
        scores = jnp.where(visible, scores, masked_value)
        peak = jnp.max(scores, axis=1, keepdims=True)
        weights = jnp.exp(scores - peak)
        probs = weights / jnp.sum(weights, axis=1, keepdims=True)
        grad_probs = jnp.dot(grad_out, latent_keys.T, preferred_element_type=jnp.float32)
        delta = jnp.sum(probs * grad_probs, axis=1, keepdims=True)
        grad_scores = (probs * (grad_probs - delta)).astype(jnp.bfloat16)
        probs_half = probs.astype(jnp.bfloat16)
        grad_query = (jnp.dot(grad_scores, keys, preferred_element_type=jnp.float32) * softmax_scale).astype(jnp.bfloat16)
        grad_key = jnp.dot(grad_scores.T, query, preferred_element_type=jnp.float32) * softmax_scale
        grad_value = jnp.dot(probs_half.T, grad_out, preferred_element_type=jnp.float32)
        grad_key = grad_key + jnp.pad(grad_value, ((0, 0), (0, ROPE)))
        return total + grad_key, grad_query

    start_total = jnp.zeros((SEQ, KDIM), jnp.float32)
    total, grad_heads = lax.scan(per_head, start_total, (jnp.swapaxes(queries, 0, 1), jnp.swapaxes(dout, 0, 1)))
    return jnp.swapaxes(grad_heads, 0, 1), total
```

```python
import functools

import jax
import jax.numpy as jnp
from jax import lax
from jax.experimental import pallas as pl
from jax.experimental.pallas import tpu as pltpu
from jax.sharding import PartitionSpec as P

SCALE = 0.1352
LOG2E = 1.4426950408889634
EXP_SCALE = SCALE * LOG2E
NEG = -1e30
LAT = 512
MESH = pl.DeviceIdType.MESH
BF16, F32 = jnp.bfloat16, jnp.float32


def dot_nt(a, b):
    return lax.dot_general(a, b, (((1,), (1,)), ((), ())), preferred_element_type=F32)


def dot_tn(a, b):
    return lax.dot_general(a, b, (((0,), (0,)), ((), ())), preferred_element_type=F32)


def dot(a, b):
    return jnp.dot(a, b, preferred_element_type=F32)


def aligned(index, size):
    return pl.ds(pl.multiple_of(index * size, size), size)


def where_am_i():
    ctx, head = lax.axis_index("ctx"), lax.axis_index("head")
    return ctx // 8, lax.rem(ctx // 2, 4), lax.rem(ctx, 2), head // 4, lax.rem(head, 4)


def place(y_hi, x, core, y_lo, z):
    return {"ctx": y_hi * 8 + x * 2 + core, "head": y_lo * 4 + z}


def greet(peers):
    barrier = pltpu.get_barrier_semaphore()
    for peer in peers:
        pl.semaphore_signal(barrier, inc=1, device_id=peer, device_id_type=MESH)
    pl.semaphore_wait(barrier, len(peers))


def attention_kernel(
    sizes, order, own_ref, q_hbm, do_hbm, dq_hbm, dk_hbm,
    keys, q_ref, do_ref, sbuf, dpbuf, pt, dst, dk_buf, dq_buf,
    in_sem, send_sem, recv_sem, pass_sem, mate_sem, dk_sem, dq_sem,
):
    shard, rows, tile, chunk = sizes
    half = shard // 2
    n_keys = keys.shape[0]
    n_tiles, n_chunks, n_groups = rows // tile, n_keys // chunk, n_keys // half
    heads = rows // shard
    y_hi, x, core, y_lo, z = where_am_i()
    ctx = lax.axis_index("ctx")

    q_in = pltpu.make_async_copy(q_hbm, q_ref, in_sem.at[0])
    do_in = pltpu.make_async_copy(do_hbm, do_ref, in_sem.at[1])
    own_in = pltpu.make_async_copy(own_ref, keys.at[aligned(ctx, shard)], in_sem.at[2])
    own_in.start()
    q_in.start()
    do_in.start()

    mate = place(y_hi, x, 1 - core, y_lo, z)
    steps = [(0, 1), (0, 3), (1, 0), (0, 2), (1, 1), (1, 3), (1, 2)]

    def peer_of(dy, dx):
        there = (y_hi + dy) % 2, lax.rem(x + dx, 4)
        return place(*there, core, (y_lo + dy) % 2, z)

    def slot_from(dy, dx):
        return ((y_hi + dy) % 2) * 8 + lax.rem(x + 4 - dx, 4) * 2 + core

    greet([mate] + [peer_of(*step) for step in steps])
    own_in.wait()
    own_slot = keys.at[aligned(ctx, shard)]
    sends = []
    for n, step in enumerate(steps):
        sends.append(pltpu.make_async_remote_copy(
            src_ref=own_slot, dst_ref=own_slot, send_sem=send_sem.at[n], recv_sem=recv_sem.at[n],
            device_id=peer_of(*step), device_id_type=MESH))
    passes = []
    for n in range(len(steps) + 1):
        slot = keys.at[aligned(ctx if n == 0 else slot_from(*steps[n - 1]), shard)]
        passes.append(pltpu.make_async_remote_copy(
            src_ref=slot, dst_ref=slot, send_sem=pass_sem.at[n], recv_sem=mate_sem.at[n],
            device_id=mate, device_id_type=MESH))
    for send in sends:
        send.start()
    passes[0].start()
    for n in range(len(steps)):
        sends[n].wait_recv()
        passes[n + 1].start()
    q_in.wait()
    do_in.wait()
    for copy in passes:
        copy.wait_recv()

    pos_a, pos_b = order[2 * ctx], order[2 * ctx + 1]
    half_rows = rows // 2

    def lane_rows(t):
        return t * tile + lax.broadcasted_iota(jnp.int32, (1, tile), 1)

    def row_pos(t):
        return jnp.where(lane_rows(t) < half_rows, pos_a, pos_b)

    def fold(value, how):
        return how(value.reshape(value.shape[0] // 8, 8, tile), axis=0)

    def scores(t, slot):
        pos = row_pos(t)
        best = jnp.full((8, tile), NEG, F32)
        s = dot_nt(keys[...], q_ref[aligned(t, tile), :])
        sbuf[slot] = s
        for g in range(n_groups):
            top = fold(s[g * half:(g + 1) * half], jnp.max)
            best = jnp.maximum(best, jnp.where(order[g] < pos, top, NEG))
        return best

    def diagonal(t, slot, best):
        own = aligned(ctx, shard)
        lanes = lane_rows(t)
        late = lanes >= half_rows
        offset = jnp.where(late, lanes - half_rows, lanes) // heads
        key = lax.broadcasted_iota(jnp.int32, (shard, 1), 0)
        key_late = key >= half
        key_off = jnp.where(key_late, key - half, key)
        same = key_late == late
        s = sbuf[slot, own, :]
        s = jnp.where(same & (key_off > offset), NEG, s)
        sbuf[slot, own, :] = s
        return jnp.maximum(best, fold(jnp.where(same, s, NEG), jnp.max))

    def weigh(t, slot, best):
        pos = row_pos(t)
        top = jnp.max(best, axis=0, keepdims=True) * EXP_SCALE
        total = jnp.zeros((8, tile), F32)
        mixed = jnp.zeros((8, tile), F32)
        for g in range(n_groups):
            span = pl.ds(g * half, half)
            shift = jnp.where(order[g] <= pos, top, -NEG)
            e = jnp.exp2(sbuf[slot, span, :] * EXP_SCALE - shift)
            sbuf[slot, span, :] = e
            total += fold(e, jnp.sum)
            mixed += fold(e * dpbuf[span, :], jnp.sum)
        scale = 1.0 / jnp.sum(total, axis=0, keepdims=True)
        return scale, jnp.sum(mixed, axis=0, keepdims=True) * scale

    def settle(t, slot, scale, delta):
        out = aligned(t, tile)
        p = sbuf[slot] * scale
        ds = p * (dpbuf[...] - delta)
        pt[:, out] = p.astype(BF16)
        dst[:, out] = ds.astype(BF16)

    def grad_probs(t):
        dpbuf[...] = dot_nt(keys[:, :LAT], do_ref[aligned(t, tile), :])

    best = diagonal(0, 0, scores(0, 0))
    grad_probs(0)

    def one_tile(t, best):
        slot = lax.rem(t, 2)
        later = scores(t + 1, 1 - slot)
        scale, delta = weigh(t, slot, best)
        later = diagonal(t + 1, 1 - slot, later)
        settle(t, slot, scale, delta)
        grad_probs(t + 1)
        return later

    best = lax.fori_loop(0, n_tiles - 1, one_tile, best)
    last = n_tiles - 1
    scale, delta = weigh(last, last % 2, best)
    settle(last, last % 2, scale, delta)

    def dk_out(i):
        return pltpu.make_async_copy(dk_buf.at[lax.rem(i, 2)], dk_hbm.at[aligned(i, chunk)], dk_sem.at[i])

    def dq_out(t):
        return pltpu.make_async_copy(dq_buf.at[lax.rem(t, 2)], dq_hbm.at[aligned(t, tile)], dq_sem.at[t])

    def key_chunk(i, carry):
        @pl.when(i >= 2)
        def _():
            dk_out(i - 2).wait()

        span = aligned(i, chunk)
        a = dot(dst[span, :], q_ref[...]) * SCALE
        b = dot(pt[span, :], do_ref[...])
        dk_buf[lax.rem(i, 2), :, :LAT] = (a[:, :LAT] + b).astype(BF16)
        dk_buf[lax.rem(i, 2), :, LAT:] = a[:, LAT:].astype(BF16)
        dk_out(i).start()
        return carry

    lax.fori_loop(0, n_chunks, key_chunk, 0)

    def query_tile(t, carry):
        @pl.when(t >= 2)
        def _():
            dq_out(t - 2).wait()

        dq_buf[lax.rem(t, 2)] = (dot_tn(dst[:, aligned(t, tile)], keys[...]) * SCALE).astype(BF16)
        dq_out(t).start()
        return carry

    lax.fori_loop(0, n_tiles, query_tile, 0)

    for send in sends:
        send.wait_send()
    for copy in passes:
        copy.wait_send()
    for i in (n_chunks - 2, n_chunks - 1):
        dk_out(i).wait()
    for t in (n_tiles - 2, n_tiles - 1):
        dq_out(t).wait()


def reduce_kernel(
    part, out_ref, mated, sums, x_far, z_far, a0, a1, z_near, x_near, part_y, from_y, part_t, from_t, final, from_z,
    mate_s, mate_r, x1_s, x1_r, z1_s, z1_r, x2_s, x2_r, z2_s, z2_r, y_s, y_r, t_s, t_r, g_s, g_r,
):
    shard, win = sums.shape[1], a0.shape[1]
    y_hi, x, core, y_lo, z = where_am_i()
    mate = place(y_hi, x, 1 - core, y_lo, z)
    xs = [lax.rem(x + d, 4) for d in range(4)]
    zs = [lax.rem(z + d, 4) for d in range(4)]
    x_peer = [place(y_hi, xs[d], core, y_lo, z) for d in range(4)]
    z_peer = [place(y_hi, x, core, y_lo, zs[d]) for d in range(4)]
    partner = place(1 - y_hi, x, core, 1 - y_lo, z)
    twin = place(y_hi, x, core, 1 - y_lo, z)
    greet([mate, partner, twin] + x_peer[1:] + z_peer[1:])

    def start_of(q):
        first = jnp.where(q == 0, 0, jnp.where(q == 1, 64, jnp.where(q == 2, 112, 160)))
        return pl.ds(pl.multiple_of(first, 16), win)

    def remote(src, dst, send, recv, device):
        return pltpu.make_async_remote_copy(
            src_ref=src, dst_ref=dst, send_sem=send, recv_sem=recv, device_id=device, device_id_type=MESH)

    pending = []

    def go(copy):
        copy.start()
        pending.append(copy)
        return copy

    order = [(g // 2) + 4 * (1 - g % 2) for g in range(8)]
    first = {g: go(remote(part.at[aligned(g * 2 + 1 - core, shard)], mated.at[g], mate_s.at[g], mate_r.at[g], mate)) for g in order}
    x1, z1 = [], []
    for g in order:
        first[g].wait_recv()
        own = part[aligned(g * 2 + core, shard), :].astype(F32)
        sums[g] = (own + mated[g].astype(F32)).astype(BF16)
        if g < 4:
            for d in (1, 3, 2):
                z1.append(go(remote(sums.at[g, start_of(zs[d])], z_far.at[d - 1, g], z1_s.at[d - 1, g], z1_r.at[d - 1, g], z_peer[d])))
    for d in (1, 3, 2):
        x1.append(go(remote(sums.at[4 + xs[d]], x_far.at[d - 1], x1_s.at[d - 1], x1_r.at[d - 1], x_peer[d])))

    for copy in z1:
        copy.wait_recv()
    for g in range(4):
        total = sums[g, start_of(z), :].astype(F32)
        for d in range(3):
            total += z_far[d, g].astype(F32)
        a0[g] = total.astype(BF16)
    x2 = [go(remote(a0.at[xs[d]], x_near.at[d - 1], x2_s.at[d - 1], x2_r.at[d - 1], x_peer[d])) for d in (1, 3, 2)]
    for copy in x1:
        copy.wait_recv()
    total = sums[4 + x].astype(F32)
    for d in range(3):
        total += x_far[d].astype(F32)
    a1[...] = total.astype(BF16)
    z2 = [go(remote(a1.at[start_of(zs[d])], z_near.at[d - 1], z2_s.at[d - 1], z2_r.at[d - 1], z_peer[d])) for d in (1, 3, 2)]

    for copy in x2 + z2:
        copy.wait_recv()
    low = a0[x].astype(F32)
    high = a1[start_of(z), :].astype(F32)
    for d in range(3):
        low += x_near[d].astype(F32)
        high += z_near[d].astype(F32)
    up = y_hi == 1
    part_y[...] = jnp.where(up, low, high)
    keep = jnp.where(up, high, low)
    go(remote(part_y, from_y, y_s, y_r, partner)).wait_recv()
    mine = keep + from_y[...]
    part_t[...] = mine
    go(remote(part_t, from_t, t_s, t_r, twin)).wait_recv()
    final[...] = mine + from_t[...]
    last = [go(remote(final, from_z.at[d - 1], g_s.at[d - 1], g_r.at[d - 1], z_peer[d])) for d in (1, 3, 2)]

    for copy in last:
        copy.wait_recv()
    for q, (lo, hi) in enumerate(((0, 64), (64, 112), (112, 160), (160, 224))):
        d = lax.rem(z - q + 4, 4)
        value = final[0:hi - lo]
        for k in range(1, 4):
            value = jnp.where(d == k, from_z[k - 1, 0:hi - lo, :], value)
        out_ref[lo:hi, :] = value
    for copy in pending:
        copy.wait_send()


def per_device(block_order, queries, keys, dout):
    shard, heads, width = queries.shape
    rows = shard * heads
    seq = shard * lax.axis_size("ctx")
    tile, chunk = 256, 2 * shard
    any_spec = pl.BlockSpec(memory_space=pl.ANY)
    vmem = pl.BlockSpec(memory_space=pltpu.VMEM)
    dma = pltpu.SemaphoreType.DMA
    grad_queries, partial = pl.pallas_call(
        functools.partial(attention_kernel, (shard, rows, tile, chunk)),
        out_shape=(jax.ShapeDtypeStruct((rows, width), BF16), jax.ShapeDtypeStruct((seq, width), BF16)),
        in_specs=[pl.BlockSpec(memory_space=pltpu.SMEM), any_spec, any_spec, any_spec],
        out_specs=[any_spec, any_spec],
        scratch_shapes=[
            pltpu.VMEM((seq, width), BF16),
            pltpu.VMEM((rows, width), BF16),
            pltpu.VMEM((rows, LAT), BF16),
            pltpu.VMEM((2, seq, tile), F32),
            pltpu.VMEM((seq, tile), F32),
            pltpu.VMEM((seq, rows), BF16),
            pltpu.VMEM((seq, rows), BF16),
            pltpu.VMEM((2, chunk, width), BF16),
            pltpu.VMEM((2, tile, width), BF16),
            dma((3,)), dma((7,)), dma((7,)), dma((8,)), dma((8,)), dma((seq // chunk,)), dma((rows // tile,)),
        ],
        compiler_params=pltpu.CompilerParams(collective_id=0, has_side_effects=True, vmem_limit_bytes=63 << 20),
    )(block_order, keys, queries.reshape(rows, width), dout.reshape(rows, LAT))
    win = 64
    key_result = pl.pallas_call(
        reduce_kernel,
        out_shape=jax.ShapeDtypeStruct((shard, width), F32),
        in_specs=[vmem],
        out_specs=vmem,
        scratch_shapes=[
            pltpu.VMEM((8, shard, width), BF16), pltpu.VMEM((8, shard, width), BF16),
            pltpu.VMEM((3, shard, width), BF16), pltpu.VMEM((3, 4, win, width), BF16),
            pltpu.VMEM((4, win, width), BF16), pltpu.VMEM((shard, width), BF16),
            pltpu.VMEM((3, win, width), BF16), pltpu.VMEM((3, win, width), BF16),
            pltpu.VMEM((win, width), F32), pltpu.VMEM((win, width), F32),
            pltpu.VMEM((win, width), F32), pltpu.VMEM((win, width), F32),
            pltpu.VMEM((win, width), F32), pltpu.VMEM((3, win, width), F32),
            dma((8,)), dma((8,)), dma((3,)), dma((3,)), dma((3, 4)), dma((3, 4)), dma((3,)), dma((3,)),
            dma((3,)), dma((3,)), dma, dma, dma, dma, dma((3,)), dma((3,)),
        ],
        compiler_params=pltpu.CompilerParams(collective_id=1, has_side_effects=True, vmem_limit_bytes=40 << 20),
    )(partial)
    return grad_queries.reshape(shard, heads, width), key_result


def solution(mesh):
    placed = (P(), P("ctx", "head", None), P("ctx", None), P("ctx", "head", None))
    return jax.shard_map(
        per_device,
        mesh=mesh,
        in_specs=placed,
        out_specs=(P("ctx", "head", None), P("ctx", None)),
        check_vma=False,
    )
```

```python
import functools

import jax
import jax.numpy as jnp
from jax import lax
from jax.experimental import pallas as pl
from jax.experimental.pallas import tpu as pltpu
from jax.sharding import PartitionSpec as P

SCALE = 0.1352
LOG2E = 1.4426950408889634
EXP_SCALE = SCALE * LOG2E
NEG = -1e30
LAT = 512
STEP = 896
MESH = pl.DeviceIdType.MESH
BF16, F32 = jnp.bfloat16, jnp.float32


def dot_nt(a, b):
    return lax.dot_general(a, b, (((1,), (1,)), ((), ())), preferred_element_type=F32)


def dot_tn(a, b):
    return lax.dot_general(a, b, (((0,), (0,)), ((), ())), preferred_element_type=F32)


def dot(a, b):
    return jnp.dot(a, b, preferred_element_type=F32)


def aligned(index, size):
    return pl.ds(pl.multiple_of(index * size, size), size)


def where_am_i():
    ctx, head = lax.axis_index("ctx"), lax.axis_index("head")
    return ctx // 8, lax.rem(ctx // 2, 4), lax.rem(ctx, 2), head // 4, lax.rem(head, 4)


def place(y_hi, x, core, y_lo, z):
    return {"ctx": y_hi * 8 + x * 2 + core, "head": y_lo * 4 + z}


def greet(peers):
    barrier = pltpu.get_barrier_semaphore()
    for peer in peers:
        pl.semaphore_signal(barrier, inc=1, device_id=peer, device_id_type=MESH)
    pl.semaphore_wait(barrier, len(peers))


def attention_kernel(
    sizes, order, own_ref, q_hbm, do_hbm, dq_hbm, dk_ref,
    keys, q_ref, do_ref, sbuf, dpbuf, pt, dst, dq_buf,
    own_part, give, mated, sums, x_fwd, x_full, z_fwd, z_near, z_full, a0, a1, z_two, x_two, halves, from_y, final, from_z,
    in_sem, send_sem, recv_sem, pass_sem, mate_sem, dq_sem,
    m_s, m_r, xf_s, xf_r, xn_s, xn_r, zf_s, zf_r, zn_s, zn_r, x2_s, x2_r, z2_s, z2_r, y_s, y_r, g_s, g_r,
):
    shard, rows, tile, chunk, win = sizes
    half = shard // 2
    n_keys = keys.shape[0]
    n_tiles, n_groups = rows // tile, n_keys // half
    heads = rows // shard
    y_hi, x, core, y_lo, z = where_am_i()
    ctx = lax.axis_index("ctx")

    q_in = pltpu.make_async_copy(q_hbm, q_ref, in_sem.at[0])
    do_in = pltpu.make_async_copy(do_hbm, do_ref, in_sem.at[1])
    own_in = pltpu.make_async_copy(own_ref, keys.at[aligned(ctx, shard)], in_sem.at[2])
    own_in.start()
    q_in.start()
    do_in.start()

    mate = place(y_hi, x, 1 - core, y_lo, z)
    steps = [(0, 1), (0, 3), (1, 0), (0, 2), (1, 1), (1, 3), (1, 2)]

    def peer_of(dy, dx):
        there = (y_hi + dy) % 2, lax.rem(x + dx, 4)
        return place(*there, core, (y_lo + dy) % 2, z)

    def slot_from(dy, dx):
        return ((y_hi + dy) % 2) * 8 + lax.rem(x + 4 - dx, 4) * 2 + core

    x_peer = [place(y_hi, lax.rem(x + d, 4), core, y_lo, z) for d in range(4)]
    z_peer = [place(y_hi, x, core, y_lo, lax.rem(z + d, 4)) for d in range(4)]
    twin = place(y_hi, x, core, 1 - y_lo, z)
    across = [twin, place(1 - y_hi, x, core, 1 - y_lo, z), place(1 - y_hi, x, core, y_lo, z)]
    greet([mate, across[0], across[2]] + z_peer[1:] + [peer_of(*step) for step in steps])
    own_in.wait()
    own_slot = keys.at[aligned(ctx, shard)]
    sends = []
    for n, step in enumerate(steps):
        sends.append(pltpu.make_async_remote_copy(
            src_ref=own_slot, dst_ref=own_slot, send_sem=send_sem.at[n], recv_sem=recv_sem.at[n],
            device_id=peer_of(*step), device_id_type=MESH))
    passes = []
    for n in range(len(steps) + 1):
        slot = keys.at[aligned(ctx if n == 0 else slot_from(*steps[n - 1]), shard)]
        passes.append(pltpu.make_async_remote_copy(
            src_ref=slot, dst_ref=slot, send_sem=pass_sem.at[n], recv_sem=mate_sem.at[n],
            device_id=mate, device_id_type=MESH))
    for send in sends:
        send.start()
    passes[0].start()
    for n in range(len(steps)):
        sends[n].wait_recv()
        passes[n + 1].start()
    q_in.wait()
    do_in.wait()
    for copy in passes:
        copy.wait_recv()

    pos_a, pos_b = order[2 * ctx], order[2 * ctx + 1]
    half_rows = rows // 2

    def lane_rows(t):
        return t * tile + lax.broadcasted_iota(jnp.int32, (1, tile), 1)

    def row_pos(t):
        return jnp.where(lane_rows(t) < half_rows, pos_a, pos_b)

    def fold(value, how):
        return how(value.reshape(value.shape[0] // 8, 8, tile), axis=0)

    def scores(t, slot):
        pos = row_pos(t)
        best = jnp.full((8, tile), NEG, F32)
        for m in range(0, n_keys, STEP):
            s = dot_nt(keys[m:m + STEP, :], q_ref[aligned(t, tile), :])
            sbuf[slot, m:m + STEP, :] = s
            for g in range(STEP // half):
                top = fold(s[g * half:(g + 1) * half], jnp.max)
                best = jnp.maximum(best, jnp.where(order[m // half + g] < pos, top, NEG))
        return best

    def diagonal(t, slot, best):
        own = aligned(ctx, shard)
        lanes = lane_rows(t)
        late = lanes >= half_rows
        offset = jnp.where(late, lanes - half_rows, lanes) // heads
        key = lax.broadcasted_iota(jnp.int32, (shard, 1), 0)
        key_late = key >= half
        key_off = jnp.where(key_late, key - half, key)
        same = key_late == late
        s = sbuf[slot, own, :]
        s = jnp.where(same & (key_off > offset), NEG, s)
        sbuf[slot, own, :] = s
        return jnp.maximum(best, fold(jnp.where(same, s, NEG), jnp.max))

    def weigh(t, slot, best):
        pos = row_pos(t)
        top = jnp.max(best, axis=0, keepdims=True) * EXP_SCALE
        total = jnp.zeros((8, tile), F32)
        mixed = jnp.zeros((8, tile), F32)
        for g in range(n_groups):
            span = pl.ds(g * half, half)
            shift = jnp.where(order[g] <= pos, top, -NEG)
            e = jnp.exp2(sbuf[slot, span, :] * EXP_SCALE - shift)
            sbuf[slot, span, :] = e
            total += fold(e, jnp.sum)
            mixed += fold(e * dpbuf[span, :], jnp.sum)
        scale = 1.0 / jnp.sum(total, axis=0, keepdims=True)
        return scale, jnp.sum(mixed, axis=0, keepdims=True) * scale

    def settle(t, slot, scale, delta):
        out = aligned(t, tile)
        for g in range(n_groups):
            span = pl.ds(g * half, half)
            p = sbuf[slot, span, :] * scale
            ds = p * (dpbuf[span, :] - delta)
            pt[span, out] = p.astype(BF16)
            dst[span, out] = ds.astype(BF16)

    def grad_probs(t):
        for m in range(0, n_keys, STEP):
            dpbuf[m:m + STEP, :] = dot_nt(keys[m:m + STEP, :LAT], do_ref[aligned(t, tile), :])

    best = diagonal(0, 0, scores(0, 0))
    grad_probs(0)

    def one_tile(t, best):
        slot = lax.rem(t, 2)
        scale, delta = weigh(t, slot, best)
        later = scores(t + 1, 1 - slot)
        settle(t, slot, scale, delta)
        grad_probs(t + 1)
        later = diagonal(t + 1, 1 - slot, later)
        return later

    best = lax.fori_loop(0, n_tiles - 1, one_tile, best)
    last = n_tiles - 1
    scale, delta = weigh(last, last % 2, best)
    settle(last, last % 2, scale, delta)

    def dq_out(t):
        return pltpu.make_async_copy(dq_buf.at[lax.rem(t, 2)], dq_hbm.at[aligned(t, tile)], dq_sem.at[t])

    def remote(src, dst, send, recv, device):
        return pltpu.make_async_remote_copy(
            src_ref=src, dst_ref=dst, send_sem=send, recv_sem=recv, device_id=device, device_id_type=MESH)

    def window(q):
        first = jnp.where(q == 0, 0, jnp.where(q == 1, 64, jnp.where(q == 2, 112, 160)))
        return pl.multiple_of(first, 16)

    def to_mate(g):
        return remote(give.at[g], mated.at[g], m_s.at[g], m_r.at[g], mate)

    def x_half(side, g):
        span = pl.ds(side * half, half)
        return remote(sums.at[g, span], x_fwd.at[side], xf_s.at[side], xf_r.at[side], x_peer[1 + 2 * side])

    def x_whole(side, g):
        return remote(sums.at[g], x_full.at[side], xn_s.at[side], xn_r.at[side], x_peer[1 + 2 * side])

    def z_half(side, g):
        span = pl.ds(window(lax.rem(z + 2, 4)) + side * (win // 2), win // 2)
        return remote(sums.at[g, span], z_fwd.at[side, g], zf_s.at[side, g], zf_r.at[side, g], z_peer[1 + 2 * side])

    def z_whole(side, g):
        return remote(z_near.at[side, g], z_full.at[side, g], zn_s.at[side, g], zn_r.at[side, g], z_peer[1 + 2 * side])

    def key_chunk(g, slot):
        for part, kind in ((core, 0), (1 - core, 1)):
            span = aligned(g * 2 + part, shard)
            a = dot(dst[span, :], q_ref[...]) * SCALE
            b = dot(pt[span, :], do_ref[...])
            if kind == 0:
                own_part[slot, :, :LAT] = a[:, :LAT] + b
                own_part[slot, :, LAT:] = a[:, LAT:]
            else:
                give[g, :, :LAT] = (a[:, :LAT] + b).astype(BF16)
                give[g, :, LAT:] = a[:, LAT:].astype(BF16)
        to_mate(g).start()

    def chip_sum(g, slot):
        to_mate(g).wait_recv()
        sums[g] = (own_part[slot] + mated[g].astype(F32)).astype(BF16)

    def z_first(g):
        chip_sum(g, 0)
        z_half(0, g).start()
        z_half(1, g).start()

    def z_second(g):
        for side in range(2):
            base = window(lax.rem(z + 1 + 2 * side, 4))
            near = pl.ds(base + side * (win // 2), win // 2)
            plain = pl.ds(base + (1 - side) * (win // 2), win // 2)
            z_half(side, g).wait_recv()
            mixed = sums[g, near, :].astype(F32) + z_fwd[side, g].astype(F32)
            z_near[side, g, pl.ds(side * (win // 2), win // 2), :] = mixed.astype(BF16)
            z_near[side, g, pl.ds((1 - side) * (win // 2), win // 2), :] = sums[g, plain, :]
            z_whole(side, g).start()

    def column(k):
        return lax.rem(x + jnp.where(k == 0, 2, jnp.where(k == 1, 1, jnp.where(k == 2, 3, 0))), 4)

    def chunk_pair(k, carry):
        col = column(k)
        before = column(lax.rem(k + 3, 4))
        key_chunk(4 + col, 1)

        @pl.when(k > 0)
        def _():
            z_first(before)

        key_chunk(col, 0)
        chip_sum(4 + col, 1)

        @pl.when(k == 0)
        def _():
            x_half(0, 4 + col).start()
            x_half(1, 4 + col).start()

        for side in range(2):
            @pl.when(k == 1 + side)
            def _():
                x_half(side, 4 + col).wait_recv()
                span = pl.ds(side * half, half)
                mixed = sums[4 + col, span, :].astype(F32) + x_fwd[side].astype(F32)
                sums[4 + col, span, :] = mixed.astype(BF16)
                x_whole(side, 4 + col).start()

        @pl.when(k > 0)
        def _():
            z_second(before)

        return carry

    lax.fori_loop(0, 4, chunk_pair, 0)
    z_first(x)

    def second_x(d):
        return remote(a0.at[lax.rem(x + d, 4)], x_two.at[d - 1], x2_s.at[d - 1], x2_r.at[d - 1], x_peer[d])

    def second_z(d):
        span = pl.ds(window(lax.rem(z + d, 4)), win)
        return remote(a1.at[span], z_two.at[d - 1], z2_s.at[d - 1], z2_r.at[d - 1], z_peer[d])

    def across_y(n):
        return remote(halves.at[y_hi if n == 0 else 1 - y_hi], from_y.at[n], y_s.at[n], y_r.at[n], across[n])

    def spread(d):
        return remote(final, from_z.at[d - 1], g_s.at[d - 1], g_r.at[d - 1], z_peer[d])

    def stage_two():
        own_window = pl.ds(window(z), win)

        def gather_z(col, carry):
            total = sums[col, own_window, :].astype(F32)
            for side in range(2):
                z_whole(side, col).wait_recv()
                total += z_full[side, col].astype(F32)
            a0[col] = total.astype(BF16)
            return carry

        lax.fori_loop(0, 4, gather_z, 0)
        total = sums[4 + x].astype(F32)
        for side in range(2):
            x_whole(side, 4 + x).wait_recv()
            total += x_full[side].astype(F32)
        a1[...] = total.astype(BF16)
        for d in (2, 1, 3):
            second_x(d).start()
            second_z(d).start()

    def stage_three():
        low = a0[x].astype(F32)
        high = a1[pl.ds(window(z), win), :].astype(F32)
        for d in (1, 3, 2):
            second_x(d).wait_recv()
            second_z(d).wait_recv()
        for d in (1, 2, 3):
            low += x_two[d - 1].astype(F32)
            high += z_two[d - 1].astype(F32)
        halves[0] = low.astype(BF16)
        halves[1] = high.astype(BF16)
        for n in (2, 1, 0):
            across_y(n).start()

    def stage_four():
        for n in range(3):
            across_y(n).wait_recv()
        near = halves[y_hi].astype(F32) + from_y[0].astype(F32)
        final[...] = (near + (from_y[1].astype(F32) + from_y[2].astype(F32))).astype(BF16)
        for d in (2, 1, 3):
            spread(d).start()

    def query_tile(t, carry):
        @pl.when(t >= 2)
        def _():
            dq_out(t - 2).wait()

        dq_buf[lax.rem(t, 2)] = (dot_tn(dst[:, aligned(t, tile)], keys[...]) * SCALE).astype(BF16)
        dq_out(t).start()
        for when, stage in ((0, lambda: z_second(x)), (2, stage_two), (4, stage_three), (6, stage_four)):
            pl.when(t == when)(stage)
        return carry

    lax.fori_loop(0, n_tiles, query_tile, 0)

    for d in (1, 3, 2):
        spread(d).wait_recv()
    for q, (lo, hi) in enumerate(((0, 64), (64, 112), (112, 160), (160, 224))):
        d = lax.rem(z - q + 4, 4)
        value = final[0:hi - lo].astype(F32)
        for k in range(1, 4):
            value = jnp.where(d == k, from_z[k - 1, 0:hi - lo, :].astype(F32), value)
        dk_ref[lo:hi, :] = value

    for send in sends:
        send.wait_send()
    for copy in passes:
        copy.wait_send()
    for t in (n_tiles - 2, n_tiles - 1):
        dq_out(t).wait()

    def drain(g, carry):
        to_mate(g).wait_send()
        to_mate(4 + g).wait_send()
        for side in range(2):
            z_half(side, g).wait_send()
            z_whole(side, g).wait_send()
        return carry

    lax.fori_loop(0, 4, drain, 0)
    for side in range(2):
        x_half(side, 4 + x).wait_send()
        x_whole(side, 4 + x).wait_send()
    for d in (1, 2, 3):
        second_x(d).wait_send()
        second_z(d).wait_send()
        spread(d).wait_send()
        across_y(d - 1).wait_send()


def per_device(block_order, queries, keys, dout):
    shard, heads, width = queries.shape
    rows = shard * heads
    seq = shard * lax.axis_size("ctx")
    tile, chunk, win = 256, 2 * shard, 64
    any_spec = pl.BlockSpec(memory_space=pl.ANY)
    dma = pltpu.SemaphoreType.DMA

    def half_type(*lead):
        return pltpu.VMEM((*lead, width), BF16)

    grad_queries, key_result = pl.pallas_call(
        functools.partial(attention_kernel, (shard, rows, tile, chunk, win)),
        out_shape=(jax.ShapeDtypeStruct((rows, width), BF16), jax.ShapeDtypeStruct((shard, width), F32)),
        in_specs=[pl.BlockSpec(memory_space=pltpu.SMEM), any_spec, any_spec, any_spec],
        out_specs=[any_spec, pl.BlockSpec(memory_space=pltpu.VMEM)],
        scratch_shapes=[
            half_type(seq), half_type(rows),
            pltpu.VMEM((rows, LAT), BF16),
            pltpu.VMEM((2, seq, tile), F32),
            pltpu.VMEM((seq, tile), F32),
            pltpu.VMEM((seq, rows), BF16),
            pltpu.VMEM((seq, rows), BF16),
            half_type(2, tile),
            pltpu.VMEM((2, shard, width), F32),
            half_type(8, shard), half_type(8, shard), half_type(8, shard),
            half_type(2, shard // 2), half_type(2, shard),
            half_type(2, 4, win // 2), half_type(2, 4, win), half_type(2, 4, win),
            half_type(4, win), half_type(shard), half_type(3, win), half_type(3, win),
            half_type(2, win), half_type(3, win), half_type(win), half_type(3, win),
            dma((3,)), dma((7,)), dma((7,)), dma((8,)), dma((8,)), dma((rows // tile,)),
            dma((8,)), dma((8,)), dma((2,)), dma((2,)), dma((2,)), dma((2,)),
            dma((2, 4)), dma((2, 4)), dma((2, 4)), dma((2, 4)),
            dma((3,)), dma((3,)), dma((3,)), dma((3,)), dma((3,)), dma((3,)), dma((3,)), dma((3,)),
        ],
        compiler_params=pltpu.CompilerParams(collective_id=0, has_side_effects=True, vmem_limit_bytes=62 << 20),
    )(block_order, keys, queries.reshape(rows, width), dout.reshape(rows, LAT))
    return grad_queries.reshape(shard, heads, width), key_result


def solution(mesh):
    placed = (P(), P("ctx", "head", None), P("ctx", None), P("ctx", "head", None))
    return jax.shard_map(
        per_device,
        mesh=mesh,
        in_specs=placed,
        out_specs=(P("ctx", "head", None), P("ctx", None)),
        check_vma=False,
    )
```

```python
import functools

import jax
import jax.numpy as jnp
from jax import lax
from jax.experimental import pallas as pl
from jax.experimental.pallas import tpu as pltpu
from jax.sharding import PartitionSpec as P

SCALE = 0.1352
LOG2E = 1.4426950408889634
EXP_SCALE = SCALE * LOG2E
NEG = -1e30
LAT = 512
STEP = 896
MESH = pl.DeviceIdType.MESH
BF16, F32 = jnp.bfloat16, jnp.float32


def dot_nt(a, b):
    return lax.dot_general(a, b, (((1,), (1,)), ((), ())), preferred_element_type=F32)


def dot_tn(a, b):
    return lax.dot_general(a, b, (((0,), (0,)), ((), ())), preferred_element_type=F32)


def dot(a, b):
    return jnp.dot(a, b, preferred_element_type=F32)


def aligned(index, size):
    return pl.ds(pl.multiple_of(index * size, size), size)


def where_am_i():
    ctx, head = lax.axis_index("ctx"), lax.axis_index("head")
    return ctx // 8, lax.rem(ctx // 2, 4), lax.rem(ctx, 2), head // 4, lax.rem(head, 4)


def place(y_hi, x, core, y_lo, z):
    return {"ctx": y_hi * 8 + x * 2 + core, "head": y_lo * 4 + z}


def greet(peers):
    barrier = pltpu.get_barrier_semaphore()
    for peer in peers:
        pl.semaphore_signal(barrier, inc=1, device_id=peer, device_id_type=MESH)
    pl.semaphore_wait(barrier, len(peers))


def attention_kernel(
    sizes, order, own_ref, q_hbm, do_hbm, dq_hbm, dk_ref,
    keys, q_ref, do_ref, sbuf, dpbuf, pt, dst, dq_buf,
    own_part, give, mated, sums, x_fwd, x_full, z_fwd, z_near, z_full, a0, a1, z_two, x_two, halves, from_y, final, from_z,
    in_sem, send_sem, recv_sem, dq_sem,
    m_s, m_r, xf_s, xf_r, xn_s, xn_r, zf_s, zf_r, zn_s, zn_r, x2_s, x2_r, z2_s, z2_r, y_s, y_r, g_s, g_r,
):
    shard, rows, tile, chunk, win = sizes
    half = shard // 2
    n_keys = keys.shape[0]
    n_tiles, n_groups = rows // tile, n_keys // half
    heads = rows // shard
    y_hi, x, core, y_lo, z = where_am_i()
    ctx = lax.axis_index("ctx")

    q_in = pltpu.make_async_copy(q_hbm, q_ref, in_sem.at[0])
    do_in = pltpu.make_async_copy(do_hbm, do_ref, in_sem.at[1])
    own_in = pltpu.make_async_copy(own_ref, keys.at[aligned(ctx, shard)], in_sem.at[2])
    own_in.start()
    q_in.start()
    do_in.start()

    mate = place(y_hi, x, 1 - core, y_lo, z)
    x_peer = [place(y_hi, lax.rem(x + d, 4), core, y_lo, z) for d in range(4)]
    z_peer = [place(y_hi, x, core, y_lo, lax.rem(z + d, 4)) for d in range(4)]
    twin = place(y_hi, x, core, 1 - y_lo, z)
    across = [twin, place(1 - y_hi, x, core, 1 - y_lo, z), place(1 - y_hi, x, core, y_lo, z)]
    greet([mate] + across + x_peer[1:] + z_peer[1:])

    win_rows = 32
    far = shard - 4 * win_rows
    counter = [0]
    sent = []

    def move(dy, dx, first, count, device):
        n = counter[0]
        counter[0] += 1
        slot = ((y_hi + dy) % 2) * 8 + lax.rem(x + dx, 4) * 2 + core
        span = keys.at[pl.ds(pl.multiple_of(slot * shard + first, 16), count)]
        copy = pltpu.make_async_remote_copy(
            src_ref=span, dst_ref=span, send_sem=send_sem.at[n], recv_sem=recv_sem.at[n],
            device_id=device, device_id_type=MESH)
        copy.start()
        sent.append(copy)
        return copy

    def await_all(copies):
        for copy in copies:
            copy.wait_recv()

    def window_at(q):
        return far + q * win_rows

    def near_x(dy):
        mine = window_at(z)
        return [[move(dy, 0, mine, win_rows, x_peer[1 + 2 * side]), move(dy, 0, 0, far, x_peer[1 + 2 * side])] for side in range(2)]

    def far_x(dy, side):
        source = 3 - 2 * side
        return [
            move(dy, source, window_at(z) + side * (win_rows // 2), win_rows // 2, x_peer[1 + 2 * side]),
            move(dy, source, side * (far // 2), far // 2, x_peer[1 + 2 * side])]

    def near_z(dy, dx):
        return [move(dy, dx, window_at(z), win_rows, z_peer[1 + 2 * side]) for side in range(2)]

    def far_z(dy, dx, arrived):
        out = []
        for side in range(2):
            arrived[side].wait_recv()
            first = window_at(lax.rem(z + 3 - 2 * side, 4)) + side * (win_rows // 2)
            out.append(move(dy, dx, first, win_rows // 2, z_peer[1 + 2 * side]))
        return out

    own_in.wait()
    over_y = [move(0, 0, window_at(z), win_rows, across[1]), move(0, 0, 0, far, across[1])]
    over_x = [near_x(0)]
    mated_keys = [move(0, 0, 0, shard, mate)]
    around, beyond = {}, {}

    def front(dy, dx):
        around[dy, dx] = near_z(dy, dx)
        mated_keys.append(move(dy, dx, 0, far, mate))

    def rest(dy, dx):
        beyond[dy, dx] = far_z(dy, dx, around[dy, dx])

    await_all(over_y)
    over_x.append(near_x(1))
    front(1, 0)
    far_over_x = []
    for dy in range(2):
        halves_x = []
        for side in range(2):
            await_all(over_x[dy][side])
            halves_x += far_x(dy, side)
            front(dy, 3 - 2 * side)
        far_over_x.append(halves_x)
        if dy == 0:
            rest(1, 0)
    rest(0, 3)
    rest(0, 1)
    await_all(far_over_x[0])
    front(0, 2)
    rest(1, 3)
    rest(1, 1)
    await_all(far_over_x[1])
    front(1, 2)
    for place_of in ((1, 0), (0, 3), (0, 1)):
        await_all(beyond[place_of])
        mated_keys.append(move(*place_of, far, 4 * win_rows, mate))
    rest(0, 2)
    rest(1, 2)
    for place_of in ((1, 3), (1, 1), (0, 2), (1, 2)):
        await_all(beyond[place_of])
        mated_keys.append(move(*place_of, far, 4 * win_rows, mate))
    q_in.wait()
    do_in.wait()
    await_all(mated_keys)

    pos_a, pos_b = order[2 * ctx], order[2 * ctx + 1]
    half_rows = rows // 2

    def lane_rows(t):
        return t * tile + lax.broadcasted_iota(jnp.int32, (1, tile), 1)

    def row_pos(t):
        return jnp.where(lane_rows(t) < half_rows, pos_a, pos_b)

    def fold(value, how):
        return how(value.reshape(value.shape[0] // 8, 8, tile), axis=0)

    step = 896

    def score_step(m, t, buf, best):
        pos = row_pos(t)
        s = dot_nt(keys[m:m + step, :], q_ref[aligned(t, tile), :])
        buf[m:m + step, :] = s
        for g in range(step // half):
            top = fold(s[g * half:(g + 1) * half], jnp.max)
            best = jnp.maximum(best, jnp.where(order[m // half + g] < pos, top, NEG))
        return best

    def diagonal(t, buf, best):
        own = aligned(ctx, shard)
        lanes = lane_rows(t)
        late = lanes >= half_rows
        offset = jnp.where(late, lanes - half_rows, lanes) // heads
        key = lax.broadcasted_iota(jnp.int32, (shard, 1), 0)
        key_late = key >= half
        key_off = jnp.where(key_late, key - half, key)
        same = key_late == late
        s = buf[own, :]
        s = jnp.where(same & (key_off > offset), NEG, s)
        buf[own, :] = s
        return jnp.maximum(best, fold(jnp.where(same, s, NEG), jnp.max))

    def weigh_step(m, t, buf, top, sums_of):
        pos = row_pos(t)
        total, mixed = sums_of
        for g in range(step // half):
            span = pl.ds(m + g * half, half)
            shift = jnp.where(order[m // half + g] <= pos, top, -NEG)
            e = jnp.exp2(buf[span, :] * EXP_SCALE - shift)
            buf[span, :] = e
            total += fold(e, jnp.sum)
            mixed += fold(e * dpbuf[span, :], jnp.sum)
        return total, mixed

    def settle_step(m, t, buf, scale, delta):
        out = aligned(t, tile)
        for g in range(step // half):
            span = pl.ds(m + g * half, half)
            p = buf[span, :] * scale
            ds = p * (dpbuf[span, :] - delta)
            pt[span, out] = p.astype(BF16)
            dst[span, out] = ds.astype(BF16)

    def probs_step(m, t):
        dpbuf[m:m + step, :] = dot_nt(keys[m:m + step, :LAT], do_ref[aligned(t, tile), :])

    spans = range(0, n_keys, step)
    lowest = jnp.full((8, tile), NEG, F32)

    def one_tile(t, now, later, best, more):
        top = jnp.max(best, axis=0, keepdims=True) * EXP_SCALE
        parts = jnp.zeros((8, tile), F32), jnp.zeros((8, tile), F32)
        next_best = lowest
        for m in spans:
            parts = weigh_step(m, t, now, top, parts)
            if more:
                next_best = score_step(m, t + 1, later, next_best)
        scale = 1.0 / jnp.sum(parts[0], axis=0, keepdims=True)
        delta = jnp.sum(parts[1], axis=0, keepdims=True) * scale
        for m in spans:
            settle_step(m, t, now, scale, delta)
            if more:
                probs_step(m, t + 1)
        return diagonal(t + 1, later, next_best) if more else None

    best = lowest
    for m in spans:
        best = score_step(m, 0, sbuf.at[0], best)
    best = diagonal(0, sbuf.at[0], best)
    for m in spans:
        probs_step(m, 0)

    def two_tiles(n, best):
        best = one_tile(2 * n, sbuf.at[0], sbuf.at[1], best, True)
        return one_tile(2 * n + 1, sbuf.at[1], sbuf.at[0], best, True)

    best = lax.fori_loop(0, (n_tiles - 1) // 2, two_tiles, best)
    one_tile(n_tiles - 1, sbuf.at[0], sbuf.at[1], best, False)

    def dq_out(t):
        return pltpu.make_async_copy(dq_buf.at[lax.rem(t, 2)], dq_hbm.at[aligned(t, tile)], dq_sem.at[t])

    def remote(src, dst, send, recv, device):
        return pltpu.make_async_remote_copy(
            src_ref=src, dst_ref=dst, send_sem=send, recv_sem=recv, device_id=device, device_id_type=MESH)

    def window(q):
        first = jnp.where(q == 0, 0, jnp.where(q == 1, 64, jnp.where(q == 2, 112, 160)))
        return pl.multiple_of(first, 16)

    def to_mate(g, k):
        slot = lax.rem(k, 2) * 2 + g // 4
        return remote(give.at[slot], mated.at[slot], m_s.at[slot], m_r.at[slot], mate)

    def x_half(side, g):
        span = pl.ds(side * half, half)
        return remote(sums.at[g, span], x_fwd.at[side], xf_s.at[side], xf_r.at[side], x_peer[1 + 2 * side])

    def x_whole(side, g):
        return remote(sums.at[g], x_full.at[side], xn_s.at[side], xn_r.at[side], x_peer[1 + 2 * side])

    def z_half(side, g):
        span = pl.ds(window(lax.rem(z + 2, 4)) + side * (win // 2), win // 2)
        return remote(sums.at[g, span], z_fwd.at[side, g], zf_s.at[side, g], zf_r.at[side, g], z_peer[1 + 2 * side])

    def z_whole(side, g):
        return remote(z_near.at[side, g], z_full.at[side, g], zn_s.at[side, g], zn_r.at[side, g], z_peer[1 + 2 * side])

    def key_chunk(g, slot, k):
        out = lax.rem(k, 2) * 2 + slot

        @pl.when(k >= 2)
        def _():
            to_mate(g, k).wait_send()

        for part, kind in ((core, 0), (1 - core, 1)):
            span = aligned(g * 2 + part, shard)
            a = dot(dst[span, :], q_ref[...]) * SCALE
            b = dot(pt[span, :], do_ref[...])
            if kind == 0:
                own_part[slot, :, :LAT] = a[:, :LAT] + b
                own_part[slot, :, LAT:] = a[:, LAT:]
            else:
                give[out, :, :LAT] = (a[:, :LAT] + b).astype(BF16)
                give[out, :, LAT:] = a[:, LAT:].astype(BF16)
        to_mate(g, k).start()

    def chip_sum(g, slot, k):
        to_mate(g, k).wait_recv()
        sums[g] = (own_part[slot] + mated[lax.rem(k, 2) * 2 + slot].astype(F32)).astype(BF16)

    def z_first(g, k):
        chip_sum(g, 0, k)
        z_half(0, g).start()
        z_half(1, g).start()

    def z_second(g):
        for side in range(2):
            base = window(lax.rem(z + 1 + 2 * side, 4))
            near = pl.ds(base + side * (win // 2), win // 2)
            plain = pl.ds(base + (1 - side) * (win // 2), win // 2)
            z_half(side, g).wait_recv()
            mixed = sums[g, near, :].astype(F32) + z_fwd[side, g].astype(F32)
            z_near[side, g, pl.ds(side * (win // 2), win // 2), :] = mixed.astype(BF16)
            z_near[side, g, pl.ds((1 - side) * (win // 2), win // 2), :] = sums[g, plain, :]
            z_whole(side, g).start()

    def column(k):
        return lax.rem(x + jnp.where(k == 0, 2, jnp.where(k == 1, 1, jnp.where(k == 2, 3, 0))), 4)

    def chunk_pair(k, carry):
        col = column(k)
        before = column(lax.rem(k + 3, 4))
        key_chunk(4 + col, 1, k)

        @pl.when(k > 0)
        def _():
            z_first(before, k - 1)

        key_chunk(col, 0, k)
        chip_sum(4 + col, 1, k)

        @pl.when(k == 0)
        def _():
            x_half(0, 4 + col).start()
            x_half(1, 4 + col).start()

        for side in range(2):
            @pl.when(k == 1 + side)
            def _():
                x_half(side, 4 + col).wait_recv()
                span = pl.ds(side * half, half)
                mixed = sums[4 + col, span, :].astype(F32) + x_fwd[side].astype(F32)
                sums[4 + col, span, :] = mixed.astype(BF16)
                x_whole(side, 4 + col).start()

        @pl.when(k > 0)
        def _():
            z_second(before)

        return carry

    lax.fori_loop(0, 4, chunk_pair, 0)
    z_first(x, 3)

    def second_x(d):
        return remote(a0.at[lax.rem(x + d, 4)], x_two.at[d - 1], x2_s.at[d - 1], x2_r.at[d - 1], x_peer[d])

    def second_z(d):
        span = pl.ds(window(lax.rem(z + d, 4)), win)
        return remote(a1.at[span], z_two.at[d - 1], z2_s.at[d - 1], z2_r.at[d - 1], z_peer[d])

    def across_y(n):
        return remote(halves.at[y_hi if n == 0 else 1 - y_hi], from_y.at[n], y_s.at[n], y_r.at[n], across[n])

    def spread(d):
        return remote(final, from_z.at[d - 1], g_s.at[d - 1], g_r.at[d - 1], z_peer[d])

    def stage_two():
        own_window = pl.ds(window(z), win)

        def gather_z(col, carry):
            total = sums[col, own_window, :].astype(F32)
            for side in range(2):
                z_whole(side, col).wait_recv()
                total += z_full[side, col].astype(F32)
            a0[col] = total.astype(BF16)
            return carry

        lax.fori_loop(0, 4, gather_z, 0)
        total = sums[4 + x].astype(F32)
        for side in range(2):
            x_whole(side, 4 + x).wait_recv()
            total += x_full[side].astype(F32)
        a1[...] = total.astype(BF16)
        for d in (2, 1, 3):
            second_x(d).start()
            second_z(d).start()

    def stage_three():
        low = a0[x].astype(F32)
        high = a1[pl.ds(window(z), win), :].astype(F32)
        for d in (1, 3, 2):
            second_x(d).wait_recv()
            second_z(d).wait_recv()
        for d in (1, 2, 3):
            low += x_two[d - 1].astype(F32)
            high += z_two[d - 1].astype(F32)
        halves[0] = low.astype(BF16)
        halves[1] = high.astype(BF16)
        for n in (2, 1, 0):
            across_y(n).start()

    def stage_four():
        for n in range(3):
            across_y(n).wait_recv()
        near = halves[y_hi].astype(F32) + from_y[0].astype(F32)
        final[...] = (near + (from_y[1].astype(F32) + from_y[2].astype(F32))).astype(BF16)
        for d in (2, 1, 3):
            spread(d).start()

    def query_tile(t, carry):
        @pl.when(t >= 2)
        def _():
            dq_out(t - 2).wait()

        dq_buf[lax.rem(t, 2)] = (dot_tn(dst[:, aligned(t, tile)], keys[...]) * SCALE).astype(BF16)
        dq_out(t).start()
        for when, stage in ((0, lambda: z_second(x)), (2, stage_two), (4, stage_three), (6, stage_four)):
            pl.when(t == when)(stage)
        return carry

    lax.fori_loop(0, n_tiles, query_tile, 0)

    for d in (1, 3, 2):
        spread(d).wait_recv()
    for q, (lo, hi) in enumerate(((0, 64), (64, 112), (112, 160), (160, 224))):
        d = lax.rem(z - q + 4, 4)
        value = final[0:hi - lo].astype(F32)
        for k in range(1, 4):
            value = jnp.where(d == k, from_z[k - 1, 0:hi - lo, :].astype(F32), value)
        dk_ref[lo:hi, :] = value

    for copy in sent:
        copy.wait_send()
    for t in (n_tiles - 2, n_tiles - 1):
        dq_out(t).wait()

    def drain(g, carry):
        to_mate(4 * lax.rem(g, 2), g // 2).wait_send()
        for side in range(2):
            z_half(side, g).wait_send()
            z_whole(side, g).wait_send()
        return carry

    lax.fori_loop(0, 4, drain, 0)
    for side in range(2):
        x_half(side, 4 + x).wait_send()
        x_whole(side, 4 + x).wait_send()
    for d in (1, 2, 3):
        second_x(d).wait_send()
        second_z(d).wait_send()
        spread(d).wait_send()
        across_y(d - 1).wait_send()


def per_device(block_order, queries, keys, dout):
    shard, heads, width = queries.shape
    rows = shard * heads
    seq = shard * lax.axis_size("ctx")
    tile, chunk, win = 256, 2 * shard, 64
    any_spec = pl.BlockSpec(memory_space=pl.ANY)
    dma = pltpu.SemaphoreType.DMA

    def half_type(*lead):
        return pltpu.VMEM((*lead, width), BF16)

    grad_queries, key_result = pl.pallas_call(
        functools.partial(attention_kernel, (shard, rows, tile, chunk, win)),
        out_shape=(jax.ShapeDtypeStruct((rows, width), BF16), jax.ShapeDtypeStruct((shard, width), F32)),
        in_specs=[pl.BlockSpec(memory_space=pltpu.SMEM), any_spec, any_spec, any_spec],
        out_specs=[any_spec, pl.BlockSpec(memory_space=pltpu.VMEM)],
        scratch_shapes=[
            half_type(seq), half_type(rows),
            pltpu.VMEM((rows, LAT), BF16),
            pltpu.VMEM((2, seq, tile), F32),
            pltpu.VMEM((seq, tile), F32),
            pltpu.VMEM((seq, rows), BF16),
            pltpu.VMEM((seq, rows), BF16),
            half_type(2, tile),
            pltpu.VMEM((2, shard, width), F32),
            half_type(4, shard), half_type(4, shard), half_type(8, shard),
            half_type(2, shard // 2), half_type(2, shard),
            half_type(2, 4, win // 2), half_type(2, 4, win), half_type(2, 4, win),
            half_type(4, win), half_type(shard), half_type(3, win), half_type(3, win),
            half_type(2, win), half_type(3, win), half_type(win), half_type(3, win),
            dma((3,)), dma((61,)), dma((61,)), dma((rows // tile,)),
            dma((4,)), dma((4,)), dma((2,)), dma((2,)), dma((2,)), dma((2,)),
            dma((2, 4)), dma((2, 4)), dma((2, 4)), dma((2, 4)),
            dma((3,)), dma((3,)), dma((3,)), dma((3,)), dma((3,)), dma((3,)), dma((3,)), dma((3,)),
        ],
        compiler_params=pltpu.CompilerParams(collective_id=0, has_side_effects=True, vmem_limit_bytes=62 << 20),
    )(block_order, keys, queries.reshape(rows, width), dout.reshape(rows, LAT))
    return grad_queries.reshape(shard, heads, width), key_result


def solution(mesh):
    placed = (P(), P("ctx", "head", None), P("ctx", None), P("ctx", "head", None))
    return jax.shard_map(
        per_device,
        mesh=mesh,
        in_specs=placed,
        out_specs=(P("ctx", "head", None), P("ctx", None)),
        check_vma=False,
    )
```

```python
import functools

import jax
import jax.numpy as jnp
from jax import lax
from jax.experimental import pallas as pl
from jax.experimental.pallas import tpu as pltpu
from jax.sharding import PartitionSpec as P

SCALE = 0.1352
LOG2E = 1.4426950408889634
EXP_SCALE = SCALE * LOG2E
NEG = -1e30
LAT = 512
STEP = 896
MESH = pl.DeviceIdType.MESH
BF16, F32 = jnp.bfloat16, jnp.float32


def dot_nt(a, b):
    return lax.dot_general(a, b, (((1,), (1,)), ((), ())), preferred_element_type=F32)


def dot_tn(a, b):
    return lax.dot_general(a, b, (((0,), (0,)), ((), ())), preferred_element_type=F32)


def dot(a, b):
    return jnp.dot(a, b, preferred_element_type=F32)


def aligned(index, size):
    return pl.ds(pl.multiple_of(index * size, size), size)


def where_am_i():
    ctx, head = lax.axis_index("ctx"), lax.axis_index("head")
    return ctx // 8, lax.rem(ctx // 2, 4), lax.rem(ctx, 2), head // 4, lax.rem(head, 4)


def place(y_hi, x, core, y_lo, z):
    return {"ctx": y_hi * 8 + x * 2 + core, "head": y_lo * 4 + z}


def greet(peers):
    barrier = pltpu.get_barrier_semaphore()
    for peer in peers:
        pl.semaphore_signal(barrier, inc=1, device_id=peer, device_id_type=MESH)
    pl.semaphore_wait(barrier, len(peers))


def attention_kernel(
    sizes, order, own_ref, q_hbm, do_hbm, dq_hbm, dk_ref,
    keys, q_ref, do_ref, sbuf, dpbuf, pt, dst, dq_buf,
    own_part, give, mated, sums, x_fwd, x_full, z_fwd, z_near, z_full, a0, a1, z_two, x_two, halves, from_y, final, from_z,
    in_sem, send_sem, recv_sem, dq_sem,
    m_s, m_r, xf_s, xf_r, xn_s, xn_r, zf_s, zf_r, zn_s, zn_r, x2_s, x2_r, z2_s, z2_r, y_s, y_r, g_s, g_r,
):
    shard, rows, tile, chunk, win = sizes
    half = shard // 2
    n_keys = keys.shape[0]
    n_tiles, n_groups = rows // tile, n_keys // half
    heads = rows // shard
    y_hi, x, core, y_lo, z = where_am_i()
    ctx = lax.axis_index("ctx")

    q_in = pltpu.make_async_copy(q_hbm, q_ref, in_sem.at[0])
    do_in = pltpu.make_async_copy(do_hbm, do_ref, in_sem.at[1])
    own_in = pltpu.make_async_copy(own_ref, keys.at[aligned(ctx, shard)], in_sem.at[2])
    own_in.start()
    q_in.start()
    do_in.start()

    mate = place(y_hi, x, 1 - core, y_lo, z)
    x_peer = [place(y_hi, lax.rem(x + d, 4), core, y_lo, z) for d in range(4)]
    z_peer = [place(y_hi, x, core, y_lo, lax.rem(z + d, 4)) for d in range(4)]
    twin = place(y_hi, x, core, 1 - y_lo, z)
    across = [twin, place(1 - y_hi, x, core, 1 - y_lo, z), place(1 - y_hi, x, core, y_lo, z)]
    greet([mate] + across + x_peer[1:] + z_peer[1:])

    win_rows = 32
    far = shard - 4 * win_rows
    counter = [0]
    sent = []

    def move(dy, dx, first, count, device):
        n = counter[0]
        counter[0] += 1
        slot = ((y_hi + dy) % 2) * 8 + lax.rem(x + dx, 4) * 2 + core
        span = keys.at[pl.ds(pl.multiple_of(slot * shard + first, 16), count)]
        copy = pltpu.make_async_remote_copy(
            src_ref=span, dst_ref=span, send_sem=send_sem.at[n], recv_sem=recv_sem.at[n],
            device_id=device, device_id_type=MESH)
        copy.start()
        sent.append(copy)
        return copy

    def await_all(copies):
        for copy in copies:
            copy.wait_recv()

    def window_at(q):
        return far + q * win_rows

    def step_of(rows_of):
        return (window_at(z), win_rows) if rows_of == "window" else (0, far)

    def near_x(dy, rows_of):
        return [move(dy, 0, *step_of(rows_of), x_peer[1 + 2 * side]) for side in range(2)]

    def far_x(dy, rows_of, arrived):
        out = []
        for side in range(2):
            arrived[side].wait_recv()
            first, count = step_of(rows_of)
            out.append(move(dy, 3 - 2 * side, first + side * (count // 2), count // 2, x_peer[1 + 2 * side]))
        return out

    def near_z(dy, dx):
        return [move(dy, dx, window_at(z), win_rows, z_peer[1 + 2 * side]) for side in range(2)]

    def far_z(dy, dx, arrived):
        out = []
        for side in range(2):
            arrived[side].wait_recv()
            first = window_at(lax.rem(z + 3 - 2 * side, 4)) + side * (win_rows // 2)
            out.append(move(dy, dx, first, win_rows // 2, z_peer[1 + 2 * side]))
        return out

    around, beyond, mated_keys = {}, {}, []

    def round_z(*sources):
        for source in sources:
            around[source] = near_z(*source)

    def round_z_again(*sources):
        for source in sources:
            beyond[source] = far_z(*source, around[source])

    def hand_over(first, count, *sources):
        for source in sources:
            mated_keys.append(move(*source, first, count, mate))

    def hand_over_windows(*sources):
        for source in sources:
            await_all(beyond[source])
            hand_over(far, 4 * win_rows, source)

    own_in.wait()
    y_window = move(0, 0, window_at(z), win_rows, across[1])
    x_window = [near_x(0, "window")]
    y_window.wait_recv()
    x_window.append(near_x(1, "window"))
    round_z((1, 0))
    x_window_far = [far_x(0, "window", x_window[0])]
    round_z((0, 3), (0, 1))
    y_rest = move(0, 0, 0, far, across[1])
    x_rest = [near_x(0, "rest")]
    hand_over(0, shard, (0, 0))
    x_window_far.append(far_x(1, "window", x_window[1]))
    round_z((1, 3), (1, 1))
    await_all(x_window_far[0])
    round_z((0, 2))
    round_z_again((1, 0))
    await_all(x_window_far[1])
    round_z((1, 2))
    round_z_again((0, 3), (0, 1))
    y_rest.wait_recv()
    x_rest.append(near_x(1, "rest"))
    hand_over(0, far, (1, 0))
    x_rest_far = [far_x(0, "rest", x_rest[0])]
    hand_over(0, far, (0, 3), (0, 1))
    round_z_again((1, 3), (1, 1), (0, 2), (1, 2))
    hand_over_windows((1, 0), (0, 3), (0, 1))
    x_rest_far.append(far_x(1, "rest", x_rest[1]))
    hand_over(0, far, (1, 3), (1, 1))
    await_all(x_rest_far[0])
    hand_over(0, far, (0, 2))
    hand_over_windows((1, 3), (1, 1), (0, 2), (1, 2))
    await_all(x_rest_far[1])
    hand_over(0, far, (1, 2))
    q_in.wait()
    do_in.wait()
    await_all(mated_keys)

    pos_a, pos_b = order[2 * ctx], order[2 * ctx + 1]
    half_rows = rows // 2

    def lane_rows(t):
        return t * tile + lax.broadcasted_iota(jnp.int32, (1, tile), 1)

    def row_pos(t):
        return jnp.where(lane_rows(t) < half_rows, pos_a, pos_b)

    def fold(value, how):
        return how(value.reshape(value.shape[0] // 8, 8, tile), axis=0)

    step = 896

    def score_step(m, t, buf, best):
        pos = row_pos(t)
        s = dot_nt(keys[m:m + step, :], q_ref[aligned(t, tile), :])
        buf[m:m + step, :] = s
        for g in range(step // half):
            top = fold(s[g * half:(g + 1) * half], jnp.max)
            best = jnp.maximum(best, jnp.where(order[m // half + g] < pos, top, NEG))
        return best

    def diagonal(t, buf, best):
        own = aligned(ctx, shard)
        lanes = lane_rows(t)
        late = lanes >= half_rows
        offset = jnp.where(late, lanes - half_rows, lanes) // heads
        key = lax.broadcasted_iota(jnp.int32, (shard, 1), 0)
        key_late = key >= half
        key_off = jnp.where(key_late, key - half, key)
        same = key_late == late
        s = buf[own, :]
        s = jnp.where(same & (key_off > offset), NEG, s)
        buf[own, :] = s
        return jnp.maximum(best, fold(jnp.where(same, s, NEG), jnp.max))

    def weigh_step(m, t, buf, top, sums_of):
        pos = row_pos(t)
        total, mixed = sums_of
        for g in range(step // half):
            span = pl.ds(m + g * half, half)
            shift = jnp.where(order[m // half + g] <= pos, top, -NEG)
            e = jnp.exp2(buf[span, :] * EXP_SCALE - shift)
            buf[span, :] = e
            total += fold(e, jnp.sum)
            mixed += fold(e * dpbuf[span, :], jnp.sum)
        return total, mixed

    def settle_step(m, t, buf, scale, delta):
        out = aligned(t, tile)
        for g in range(step // half):
            span = pl.ds(m + g * half, half)
            p = buf[span, :] * scale
            ds = p * (dpbuf[span, :] - delta)
            pt[span, out] = p.astype(BF16)
            dst[span, out] = ds.astype(BF16)

    def probs_step(m, t):
        dpbuf[m:m + step, :] = dot_nt(keys[m:m + step, :LAT], do_ref[aligned(t, tile), :])

    spans = range(0, n_keys, step)
    lowest = jnp.full((8, tile), NEG, F32)

    def one_tile(t, now, later, best, more):
        top = jnp.max(best, axis=0, keepdims=True) * EXP_SCALE
        parts = jnp.zeros((8, tile), F32), jnp.zeros((8, tile), F32)
        next_best = lowest
        for m in spans:
            parts = weigh_step(m, t, now, top, parts)
            if more:
                next_best = score_step(m, t + 1, later, next_best)
        scale = 1.0 / jnp.sum(parts[0], axis=0, keepdims=True)
        delta = jnp.sum(parts[1], axis=0, keepdims=True) * scale
        for m in spans:
            settle_step(m, t, now, scale, delta)
            if more:
                probs_step(m, t + 1)
        return diagonal(t + 1, later, next_best) if more else None

    best = lowest
    for m in spans:
        best = score_step(m, 0, sbuf.at[0], best)
    best = diagonal(0, sbuf.at[0], best)
    for m in spans:
        probs_step(m, 0)

    def two_tiles(n, best):
        best = one_tile(2 * n, sbuf.at[0], sbuf.at[1], best, True)
        return one_tile(2 * n + 1, sbuf.at[1], sbuf.at[0], best, True)

    best = lax.fori_loop(0, (n_tiles - 1) // 2, two_tiles, best)
    one_tile(n_tiles - 1, sbuf.at[0], sbuf.at[1], best, False)

    def dq_out(t):
        return pltpu.make_async_copy(dq_buf.at[lax.rem(t, 2)], dq_hbm.at[aligned(t, tile)], dq_sem.at[t])

    def remote(src, dst, send, recv, device):
        return pltpu.make_async_remote_copy(
            src_ref=src, dst_ref=dst, send_sem=send, recv_sem=recv, device_id=device, device_id_type=MESH)

    def window(q):
        first = jnp.where(q == 0, 0, jnp.where(q == 1, 64, jnp.where(q == 2, 112, 160)))
        return pl.multiple_of(first, 16)

    def to_mate(g, k):
        slot = lax.rem(k, 2) * 2 + g // 4
        return remote(give.at[slot], mated.at[slot], m_s.at[slot], m_r.at[slot], mate)

    def x_half(side, g):
        span = pl.ds(side * half, half)
        return remote(sums.at[g, span], x_fwd.at[side], xf_s.at[side], xf_r.at[side], x_peer[1 + 2 * side])

    def x_whole(side, g):
        return remote(sums.at[g], x_full.at[side], xn_s.at[side], xn_r.at[side], x_peer[1 + 2 * side])

    def z_half(side, g):
        span = pl.ds(window(lax.rem(z + 2, 4)) + side * (win // 2), win // 2)
        return remote(sums.at[g, span], z_fwd.at[side, g], zf_s.at[side, g], zf_r.at[side, g], z_peer[1 + 2 * side])

    def z_whole(side, g):
        return remote(z_near.at[side, g], z_full.at[side, g], zn_s.at[side, g], zn_r.at[side, g], z_peer[1 + 2 * side])

    def key_chunk(g, slot, k):
        out = lax.rem(k, 2) * 2 + slot

        @pl.when(k >= 2)
        def _():
            to_mate(g, k).wait_send()

        kept, given = aligned(g * 2 + core, shard), aligned(g * 2 + 1 - core, shard)
        a = dot(jnp.concatenate([dst[kept, :], dst[given, :]]), q_ref[...]) * SCALE
        b = dot(jnp.concatenate([pt[kept, :], pt[given, :]]), do_ref[...])
        own_part[slot, :, :LAT] = a[:shard, :LAT] + b[:shard]
        own_part[slot, :, LAT:] = a[:shard, LAT:]
        give[out, :, :LAT] = (a[shard:, :LAT] + b[shard:]).astype(BF16)
        give[out, :, LAT:] = a[shard:, LAT:].astype(BF16)
        to_mate(g, k).start()

    def chip_sum(g, slot, k):
        to_mate(g, k).wait_recv()
        sums[g] = (own_part[slot] + mated[lax.rem(k, 2) * 2 + slot].astype(F32)).astype(BF16)

    def z_first(g, k):
        chip_sum(g, 0, k)
        z_half(0, g).start()
        z_half(1, g).start()

    def z_second(g):
        for side in range(2):
            base = window(lax.rem(z + 1 + 2 * side, 4))
            near = pl.ds(base + side * (win // 2), win // 2)
            plain = pl.ds(base + (1 - side) * (win // 2), win // 2)
            z_half(side, g).wait_recv()
            mixed = sums[g, near, :].astype(F32) + z_fwd[side, g].astype(F32)
            z_near[side, g, pl.ds(side * (win // 2), win // 2), :] = mixed.astype(BF16)
            z_near[side, g, pl.ds((1 - side) * (win // 2), win // 2), :] = sums[g, plain, :]
            z_whole(side, g).start()

    def column(k):
        return lax.rem(x + jnp.where(k == 0, 2, jnp.where(k == 1, 1, jnp.where(k == 2, 3, 0))), 4)

    def chunk_pair(k, carry):
        col = column(k)
        before = column(lax.rem(k + 3, 4))
        @pl.when(k < 3)
        def _():
            key_chunk(4 + col, 1, k)

        @pl.when(k > 0)
        def _():
            z_first(before, k - 1)

        key_chunk(col, 0, k)
        @pl.when(k < 3)
        def _():
            chip_sum(4 + col, 1, k)

        @pl.when(k == 0)
        def _():
            x_half(0, 4 + col).start()
            x_half(1, 4 + col).start()

        for side in range(2):
            @pl.when(k == 1 + side)
            def _():
                x_half(side, 4 + col).wait_recv()
                span = pl.ds(side * half, half)
                mixed = sums[4 + col, span, :].astype(F32) + x_fwd[side].astype(F32)
                sums[4 + col, span, :] = mixed.astype(BF16)
                x_whole(side, 4 + col).start()

        @pl.when(k > 0)
        def _():
            z_second(before)

        return carry

    lax.fori_loop(0, 4, chunk_pair, 0)
    key_chunk(4 + x, 1, 3)
    z_first(x, 3)

    def second_x(d):
        return remote(a0.at[lax.rem(x + d, 4)], x_two.at[d - 1], x2_s.at[d - 1], x2_r.at[d - 1], x_peer[d])

    def second_z(d):
        span = pl.ds(window(lax.rem(z + d, 4)), win)
        return remote(a1.at[span], z_two.at[d - 1], z2_s.at[d - 1], z2_r.at[d - 1], z_peer[d])

    def across_y(n):
        return remote(halves.at[y_hi if n == 0 else 1 - y_hi], from_y.at[n], y_s.at[n], y_r.at[n], across[n])

    def spread(d):
        return remote(final, from_z.at[d - 1], g_s.at[d - 1], g_r.at[d - 1], z_peer[d])

    def stage_two():
        own_window = pl.ds(window(z), win)

        def gather_z(col, carry):
            total = sums[col, own_window, :].astype(F32)
            for side in range(2):
                z_whole(side, col).wait_recv()
                total += z_full[side, col].astype(F32)
            a0[col] = total.astype(BF16)
            return carry

        lax.fori_loop(0, 4, gather_z, 0)
        total = sums[4 + x].astype(F32)
        for side in range(2):
            x_whole(side, 4 + x).wait_recv()
            total += x_full[side].astype(F32)
        a1[...] = total.astype(BF16)
        for d in (2, 1, 3):
            second_x(d).start()
            second_z(d).start()

    def stage_three():
        low = a0[x].astype(F32)
        high = a1[pl.ds(window(z), win), :].astype(F32)
        for d in (1, 3, 2):
            second_x(d).wait_recv()
            second_z(d).wait_recv()
        for d in (1, 2, 3):
            low += x_two[d - 1].astype(F32)
            high += z_two[d - 1].astype(F32)
        halves[0] = low.astype(BF16)
        halves[1] = high.astype(BF16)
        for n in (2, 1, 0):
            across_y(n).start()

    def stage_four():
        for n in range(3):
            across_y(n).wait_recv()
        near = halves[y_hi].astype(F32) + from_y[0].astype(F32)
        final[...] = (near + (from_y[1].astype(F32) + from_y[2].astype(F32))).astype(BF16)
        for d in (2, 1, 3):
            spread(d).start()

    def last_sums():
        z_second(x)
        chip_sum(4 + x, 1, 3)

    def query_tile(t, carry):
        @pl.when(t >= 2)
        def _():
            dq_out(t - 2).wait()

        dq_buf[lax.rem(t, 2)] = (dot_tn(dst[:, aligned(t, tile)], keys[...]) * SCALE).astype(BF16)
        dq_out(t).start()
        for when, stage in ((0, last_sums), (2, stage_two), (4, stage_three), (6, stage_four)):
            pl.when(t == when)(stage)
        return carry

    lax.fori_loop(0, n_tiles, query_tile, 0)

    for d in (1, 3, 2):
        spread(d).wait_recv()
    for q, (lo, hi) in enumerate(((0, 64), (64, 112), (112, 160), (160, 224))):
        d = lax.rem(z - q + 4, 4)
        value = final[0:hi - lo].astype(F32)
        for k in range(1, 4):
            value = jnp.where(d == k, from_z[k - 1, 0:hi - lo, :].astype(F32), value)
        dk_ref[lo:hi, :] = value

    for copy in sent:
        copy.wait_send()
    for t in (n_tiles - 2, n_tiles - 1):
        dq_out(t).wait()

    def drain(g, carry):
        to_mate(4 * lax.rem(g, 2), g // 2).wait_send()
        for side in range(2):
            z_half(side, g).wait_send()
            z_whole(side, g).wait_send()
        return carry

    lax.fori_loop(0, 4, drain, 0)
    for side in range(2):
        x_half(side, 4 + x).wait_send()
        x_whole(side, 4 + x).wait_send()
    for d in (1, 2, 3):
        second_x(d).wait_send()
        second_z(d).wait_send()
        spread(d).wait_send()
        across_y(d - 1).wait_send()


def per_device(block_order, queries, keys, dout):
    shard, heads, width = queries.shape
    rows = shard * heads
    seq = shard * lax.axis_size("ctx")
    tile, chunk, win = 256, 2 * shard, 64
    any_spec = pl.BlockSpec(memory_space=pl.ANY)
    dma = pltpu.SemaphoreType.DMA

    def half_type(*lead):
        return pltpu.VMEM((*lead, width), BF16)

    grad_queries, key_result = pl.pallas_call(
        functools.partial(attention_kernel, (shard, rows, tile, chunk, win)),
        out_shape=(jax.ShapeDtypeStruct((rows, width), BF16), jax.ShapeDtypeStruct((shard, width), F32)),
        in_specs=[pl.BlockSpec(memory_space=pltpu.SMEM), any_spec, any_spec, any_spec],
        out_specs=[any_spec, pl.BlockSpec(memory_space=pltpu.VMEM)],
        scratch_shapes=[
            half_type(seq), half_type(rows),
            pltpu.VMEM((rows, LAT), BF16),
            pltpu.VMEM((2, seq, tile), F32),
            pltpu.VMEM((seq, tile), F32),
            pltpu.VMEM((seq, rows), BF16),
            pltpu.VMEM((seq, rows), BF16),
            half_type(2, tile),
            pltpu.VMEM((2, shard, width), F32),
            half_type(4, shard), half_type(4, shard), half_type(8, shard),
            half_type(2, shard // 2), half_type(2, shard),
            half_type(2, 4, win // 2), half_type(2, 4, win), half_type(2, 4, win),
            half_type(4, win), half_type(shard), half_type(3, win), half_type(3, win),
            half_type(2, win), half_type(3, win), half_type(win), half_type(3, win),
            dma((3,)), dma((61,)), dma((61,)), dma((rows // tile,)),
            dma((4,)), dma((4,)), dma((2,)), dma((2,)), dma((2,)), dma((2,)),
            dma((2, 4)), dma((2, 4)), dma((2, 4)), dma((2, 4)),
            dma((3,)), dma((3,)), dma((3,)), dma((3,)), dma((3,)), dma((3,)), dma((3,)), dma((3,)),
        ],
        compiler_params=pltpu.CompilerParams(collective_id=0, has_side_effects=True, vmem_limit_bytes=63 << 20),
    )(block_order, keys, queries.reshape(rows, width), dout.reshape(rows, LAT))
    return grad_queries.reshape(shard, heads, width), key_result


def solution(mesh):
    placed = (P(), P("ctx", "head", None), P("ctx", None), P("ctx", "head", None))
    return jax.shard_map(
        per_device,
        mesh=mesh,
        in_specs=placed,
        out_specs=(P("ctx", "head", None), P("ctx", None)),
        check_vma=False,
    )
```

```python
import functools

import jax
import jax.numpy as jnp
from jax import lax
from jax.experimental import pallas as pl
from jax.experimental.pallas import tpu as pltpu
from jax.sharding import PartitionSpec as P

SCALE = 0.1352
LOG2E = 1.4426950408889634
EXP_SCALE = SCALE * LOG2E
NEG = -1e30
LAT = 512
PIECES = 2
STEP = 896
MESH = pl.DeviceIdType.MESH
BF16, F32 = jnp.bfloat16, jnp.float32


def dot_nt(a, b):
    return lax.dot_general(a, b, (((1,), (1,)), ((), ())), preferred_element_type=F32)


def dot_tn(a, b):
    return lax.dot_general(a, b, (((0,), (0,)), ((), ())), preferred_element_type=F32)


def dot(a, b):
    return jnp.dot(a, b, preferred_element_type=F32)


def aligned(index, size):
    return pl.ds(pl.multiple_of(index * size, size), size)


def where_am_i():
    ctx, head = lax.axis_index("ctx"), lax.axis_index("head")
    return ctx // 8, lax.rem(ctx // 2, 4), lax.rem(ctx, 2), head // 4, lax.rem(head, 4)


def place(y_hi, x, core, y_lo, z):
    return {"ctx": y_hi * 8 + x * 2 + core, "head": y_lo * 4 + z}


def greet(peers):
    barrier = pltpu.get_barrier_semaphore()
    for peer in peers:
        pl.semaphore_signal(barrier, inc=1, device_id=peer, device_id_type=MESH)
    pl.semaphore_wait(barrier, len(peers))


def attention_kernel(
    sizes, order, own_ref, q_hbm, do_hbm, dq_hbm, dk_ref,
    keys, q_ref, do_ref, sbuf, dpbuf, pt, dst, dq_buf,
    own_part, give, mated, sums, x_fwd, x_full, z_fwd, z_near, z_full, a0, a1, z_two, x_two, halves, from_y, final, from_z,
    in_sem, send_sem, recv_sem, dq_sem,
    m_s, m_r, xf_s, xf_r, xn_s, xn_r, zf_s, zf_r, zn_s, zn_r, x2_s, x2_r, z2_s, z2_r, y_s, y_r, g_s, g_r,
):
    shard, rows, tile, chunk, win = sizes
    half = shard // 2
    n_keys = keys.shape[0]
    n_tiles, n_groups = rows // tile, n_keys // half
    heads = rows // shard
    y_hi, x, core, y_lo, z = where_am_i()
    ctx = lax.axis_index("ctx")

    q_in = pltpu.make_async_copy(q_hbm, q_ref, in_sem.at[0])
    do_in = pltpu.make_async_copy(do_hbm, do_ref, in_sem.at[1])
    own_in = pltpu.make_async_copy(own_ref, keys.at[aligned(ctx, shard)], in_sem.at[2])
    own_in.start()
    q_in.start()
    do_in.start()

    mate = place(y_hi, x, 1 - core, y_lo, z)
    x_peer = [place(y_hi, lax.rem(x + d, 4), core, y_lo, z) for d in range(4)]
    z_peer = [place(y_hi, x, core, y_lo, lax.rem(z + d, 4)) for d in range(4)]
    twin = place(y_hi, x, core, 1 - y_lo, z)
    across = [twin, place(1 - y_hi, x, core, 1 - y_lo, z), place(1 - y_hi, x, core, y_lo, z)]
    greet([mate] + across + x_peer[1:] + z_peer[1:])

    win_rows = 32
    far = shard - 4 * win_rows
    counter = [0]
    sent = []

    def move(dy, dx, first, count, device):
        n = counter[0]
        counter[0] += 1
        slot = ((y_hi + dy) % 2) * 8 + lax.rem(x + dx, 4) * 2 + core
        span = keys.at[pl.ds(pl.multiple_of(slot * shard + first, 16), count)]
        copy = pltpu.make_async_remote_copy(
            src_ref=span, dst_ref=span, send_sem=send_sem.at[n], recv_sem=recv_sem.at[n],
            device_id=device, device_id_type=MESH)
        copy.start()
        sent.append(copy)
        return copy

    def await_all(copies):
        for copy in copies:
            copy.wait_recv()

    def window_at(q):
        return far + q * win_rows

    def step_of(rows_of):
        return (window_at(z), win_rows) if rows_of == "window" else (0, far)

    def near_x(dy, rows_of):
        return [move(dy, 0, *step_of(rows_of), x_peer[1 + 2 * side]) for side in range(2)]

    def far_x(dy, rows_of, arrived):
        out = []
        for side in range(2):
            arrived[side].wait_recv()
            first, count = step_of(rows_of)
            out.append(move(dy, 3 - 2 * side, first + side * (count // 2), count // 2, x_peer[1 + 2 * side]))
        return out

    def near_z(dy, dx):
        return [move(dy, dx, window_at(z), win_rows, z_peer[1 + 2 * side]) for side in range(2)]

    def far_z(dy, dx, arrived):
        out = []
        for side in range(2):
            arrived[side].wait_recv()
            first = window_at(lax.rem(z + 3 - 2 * side, 4)) + side * (win_rows // 2)
            out.append(move(dy, dx, first, win_rows // 2, z_peer[1 + 2 * side]))
        return out

    around, beyond, mated_keys = {}, {}, []

    def round_z(*sources):
        for source in sources:
            around[source] = near_z(*source)

    def round_z_again(*sources):
        for source in sources:
            beyond[source] = far_z(*source, around[source])

    def hand_over(first, count, *sources):
        for source in sources:
            mated_keys.append(move(*source, first, count, mate))

    def hand_over_windows(*sources):
        for source in sources:
            await_all(beyond[source])
            hand_over(far, 4 * win_rows, source)

    own_in.wait()
    y_window = move(0, 0, window_at(z), win_rows, across[1])
    x_window = [near_x(0, "window")]
    y_window.wait_recv()
    x_window.append(near_x(1, "window"))
    round_z((1, 0))
    x_window_far = [far_x(0, "window", x_window[0])]
    round_z((0, 3), (0, 1))
    y_rest = move(0, 0, 0, far, across[1])
    x_rest = [near_x(0, "rest")]
    hand_over(0, shard, (0, 0))
    x_window_far.append(far_x(1, "window", x_window[1]))
    round_z((1, 3), (1, 1))
    await_all(x_window_far[0])
    round_z((0, 2))
    round_z_again((1, 0))
    await_all(x_window_far[1])
    round_z((1, 2))
    round_z_again((0, 3), (0, 1))
    y_rest.wait_recv()
    x_rest.append(near_x(1, "rest"))
    hand_over(0, far, (1, 0))
    x_rest_far = [far_x(0, "rest", x_rest[0])]
    hand_over(0, far, (0, 3), (0, 1))
    round_z_again((1, 3), (1, 1), (0, 2), (1, 2))
    hand_over_windows((1, 0), (0, 3), (0, 1))
    x_rest_far.append(far_x(1, "rest", x_rest[1]))
    hand_over(0, far, (1, 3), (1, 1))
    await_all(x_rest_far[0])
    hand_over(0, far, (0, 2))
    hand_over_windows((1, 3), (1, 1), (0, 2), (1, 2))
    await_all(x_rest_far[1])
    hand_over(0, far, (1, 2))
    q_in.wait()
    do_in.wait()
    await_all(mated_keys)

    pos_a, pos_b = order[2 * ctx], order[2 * ctx + 1]
    half_rows = rows // 2

    def lane_rows(t):
        return t * tile + lax.broadcasted_iota(jnp.int32, (1, tile), 1)

    def row_pos(t):
        return jnp.where(lane_rows(t) < half_rows, pos_a, pos_b)

    def fold(value, how):
        return how(value.reshape(value.shape[0] // 8, 8, tile), axis=0)

    step = 896

    def score_step(m, t, buf, best):
        pos = row_pos(t)
        s = dot_nt(keys[m:m + step, :], q_ref[aligned(t, tile), :])
        buf[m:m + step, :] = s
        for g in range(step // half):
            top = fold(s[g * half:(g + 1) * half], jnp.max)
            best = jnp.maximum(best, jnp.where(order[m // half + g] < pos, top, NEG))
        return best

    def diagonal(t, buf, best):
        own = aligned(ctx, shard)
        lanes = lane_rows(t)
        late = lanes >= half_rows
        offset = jnp.where(late, lanes - half_rows, lanes) // heads
        key = lax.broadcasted_iota(jnp.int32, (shard, 1), 0)
        key_late = key >= half
        key_off = jnp.where(key_late, key - half, key)
        same = key_late == late
        s = buf[own, :]
        s = jnp.where(same & (key_off > offset), NEG, s)
        buf[own, :] = s
        return jnp.maximum(best, fold(jnp.where(same, s, NEG), jnp.max))

    def weigh_step(m, t, buf, top, sums_of):
        pos = row_pos(t)
        total, mixed = sums_of
        for g in range(step // half):
            span = pl.ds(m + g * half, half)
            shift = jnp.where(order[m // half + g] <= pos, top, -NEG)
            e = jnp.exp2(buf[span, :] * EXP_SCALE - shift)
            buf[span, :] = e
            total += fold(e, jnp.sum)
            mixed += fold(e * dpbuf[span, :], jnp.sum)
        return total, mixed

    def settle_step(m, t, buf, scale, delta):
        out = aligned(t, tile)
        for g in range(step // half):
            span = pl.ds(m + g * half, half)
            p = buf[span, :] * scale
            ds = p * (dpbuf[span, :] - delta)
            pt[span, out] = p.astype(BF16)
            dst[span, out] = ds.astype(BF16)

    def probs_step(m, t):
        dpbuf[m:m + step, :] = dot_nt(keys[m:m + step, :LAT], do_ref[aligned(t, tile), :])

    spans = range(0, n_keys, step)
    lowest = jnp.full((8, tile), NEG, F32)

    def one_tile(t, now, later, best, more):
        top = jnp.max(best, axis=0, keepdims=True) * EXP_SCALE
        parts = jnp.zeros((8, tile), F32), jnp.zeros((8, tile), F32)
        next_best = lowest
        for m in spans:
            parts = weigh_step(m, t, now, top, parts)
            if more:
                next_best = score_step(m, t + 1, later, next_best)
        scale = 1.0 / jnp.sum(parts[0], axis=0, keepdims=True)
        delta = jnp.sum(parts[1], axis=0, keepdims=True) * scale
        for m in spans:
            settle_step(m, t, now, scale, delta)
            if more:
                probs_step(m, t + 1)
        return diagonal(t + 1, later, next_best) if more else None

    best = lowest
    for m in spans:
        best = score_step(m, 0, sbuf.at[0], best)
    best = diagonal(0, sbuf.at[0], best)
    for m in spans:
        probs_step(m, 0)

    def two_tiles(n, best):
        best = one_tile(2 * n, sbuf.at[0], sbuf.at[1], best, True)
        return one_tile(2 * n + 1, sbuf.at[1], sbuf.at[0], best, True)

    best = lax.fori_loop(0, (n_tiles - 1) // 2, two_tiles, best)
    one_tile(n_tiles - 1, sbuf.at[0], sbuf.at[1], best, False)

    def dq_out(t):
        return pltpu.make_async_copy(dq_buf.at[lax.rem(t, 2)], dq_hbm.at[aligned(t, tile)], dq_sem.at[t])

    def remote(src, dst, send, recv, device):
        return pltpu.make_async_remote_copy(
            src_ref=src, dst_ref=dst, send_sem=send, recv_sem=recv, device_id=device, device_id_type=MESH)

    def window(q):
        first = jnp.where(q == 0, 0, jnp.where(q == 1, 64, jnp.where(q == 2, 112, 160)))
        return pl.multiple_of(first, 16)

    def to_mate(g, k):
        slot = lax.rem(k, 2) * 2 + g // 4
        return remote(give.at[slot], mated.at[slot], m_s.at[slot], m_r.at[slot], mate)

    def x_half(side, g):
        span = pl.ds(side * half, half)
        return remote(sums.at[g, span], x_fwd.at[side], xf_s.at[side], xf_r.at[side], x_peer[1 + 2 * side])

    def x_whole(side, g):
        return remote(sums.at[g], x_full.at[side], xn_s.at[side], xn_r.at[side], x_peer[1 + 2 * side])

    def z_half(side, g):
        span = pl.ds(window(lax.rem(z + 2, 4)) + side * (win // 2), win // 2)
        return remote(sums.at[g, span], z_fwd.at[side, g], zf_s.at[side, g], zf_r.at[side, g], z_peer[1 + 2 * side])

    def z_whole(side, g):
        return remote(z_near.at[side, g], z_full.at[side, g], zn_s.at[side, g], zn_r.at[side, g], z_peer[1 + 2 * side])

    def key_chunk(g, slot, k):
        out = lax.rem(k, 2) * 2 + slot

        @pl.when(k >= 2)
        def _():
            to_mate(g, k).wait_send()

        kept, given = aligned(g * 2 + core, shard), aligned(g * 2 + 1 - core, shard)
        a = dot(jnp.concatenate([dst[kept, :], dst[given, :]]), q_ref[...]) * SCALE
        b = dot(jnp.concatenate([pt[kept, :], pt[given, :]]), do_ref[...])
        own_part[slot, :, :LAT] = a[:shard, :LAT] + b[:shard]
        own_part[slot, :, LAT:] = a[:shard, LAT:]
        give[out, :, :LAT] = (a[shard:, :LAT] + b[shard:]).astype(BF16)
        give[out, :, LAT:] = a[shard:, LAT:].astype(BF16)
        to_mate(g, k).start()

    def chip_sum(g, slot, k):
        to_mate(g, k).wait_recv()
        sums[g] = (own_part[slot] + mated[lax.rem(k, 2) * 2 + slot].astype(F32)).astype(BF16)

    def z_first(g, k):
        chip_sum(g, 0, k)
        z_half(0, g).start()
        z_half(1, g).start()

    def z_second(g):
        for side in range(2):
            base = window(lax.rem(z + 1 + 2 * side, 4))
            near = pl.ds(base + side * (win // 2), win // 2)
            plain = pl.ds(base + (1 - side) * (win // 2), win // 2)
            z_half(side, g).wait_recv()
            mixed = sums[g, near, :].astype(F32) + z_fwd[side, g].astype(F32)
            z_near[side, g, pl.ds(side * (win // 2), win // 2), :] = mixed.astype(BF16)
            z_near[side, g, pl.ds((1 - side) * (win // 2), win // 2), :] = sums[g, plain, :]
            z_whole(side, g).start()

    def column(k):
        return lax.rem(x + jnp.where(k == 0, 2, jnp.where(k == 1, 1, jnp.where(k == 2, 3, 0))), 4)

    def chunk_pair(k, carry):
        col = column(k)
        before = column(lax.rem(k + 3, 4))
        @pl.when(k < 3)
        def _():
            key_chunk(4 + col, 1, k)

        @pl.when(k > 0)
        def _():
            z_first(before, k - 1)

        key_chunk(col, 0, k)
        @pl.when(k < 3)
        def _():
            chip_sum(4 + col, 1, k)

        @pl.when(k == 0)
        def _():
            x_half(0, 4 + col).start()
            x_half(1, 4 + col).start()

        for side in range(2):
            @pl.when(k == 1 + side)
            def _():
                x_half(side, 4 + col).wait_recv()
                span = pl.ds(side * half, half)
                mixed = sums[4 + col, span, :].astype(F32) + x_fwd[side].astype(F32)
                sums[4 + col, span, :] = mixed.astype(BF16)
                x_whole(side, 4 + col).start()

        @pl.when(k > 0)
        def _():
            z_second(before)

        return carry

    lax.fori_loop(0, 4, chunk_pair, 0)
    key_chunk(4 + x, 1, 3)
    z_first(x, 3)

    def second_x(d):
        return remote(a0.at[lax.rem(x + d, 4)], x_two.at[d - 1], x2_s.at[d - 1], x2_r.at[d - 1], x_peer[d])

    def second_z(d):
        span = pl.ds(window(lax.rem(z + d, 4)), win)
        return remote(a1.at[span], z_two.at[d - 1], z2_s.at[d - 1], z2_r.at[d - 1], z_peer[d])

    def across_y(n):
        return remote(halves.at[y_hi if n == 0 else 1 - y_hi], from_y.at[n], y_s.at[n], y_r.at[n], across[n])

    def spread(d):
        return remote(final, from_z.at[d - 1], g_s.at[d - 1], g_r.at[d - 1], z_peer[d])

    def stage_two():
        own_window = pl.ds(window(z), win)

        def gather_z(col, carry):
            total = sums[col, own_window, :].astype(F32)
            for side in range(2):
                z_whole(side, col).wait_recv()
                total += z_full[side, col].astype(F32)
            a0[col] = total.astype(BF16)
            return carry

        lax.fori_loop(0, 4, gather_z, 0)
        total = sums[4 + x].astype(F32)
        for side in range(2):
            x_whole(side, 4 + x).wait_recv()
            total += x_full[side].astype(F32)
        a1[...] = total.astype(BF16)
        for d in (2, 1, 3):
            second_x(d).start()
            second_z(d).start()

    def stage_three():
        low = a0[x].astype(F32)
        high = a1[pl.ds(window(z), win), :].astype(F32)
        for d in (1, 3, 2):
            second_x(d).wait_recv()
            second_z(d).wait_recv()
        for d in (1, 2, 3):
            low += x_two[d - 1].astype(F32)
            high += z_two[d - 1].astype(F32)
        halves[0] = low.astype(BF16)
        halves[1] = high.astype(BF16)
        for n in (2, 1, 0):
            across_y(n).start()

    def stage_four():
        for n in range(3):
            across_y(n).wait_recv()
        near = halves[y_hi].astype(F32) + from_y[0].astype(F32)
        final[...] = (near + (from_y[1].astype(F32) + from_y[2].astype(F32))).astype(BF16)
        for d in (2, 1, 3):
            spread(d).start()

    def last_sums():
        z_second(x)
        chip_sum(4 + x, 1, 3)

    def query_tile(t, carry):
        @pl.when(t >= 2)
        def _():
            dq_out(t - 2).wait()

        dq_buf[lax.rem(t, 2)] = (dot_tn(dst[:, aligned(t, tile)], keys[...]) * SCALE).astype(BF16)
        dq_out(t).start()
        for when, stage in ((0, last_sums), (2, stage_two), (4, stage_three), (6, stage_four)):
            pl.when(t == when)(stage)
        return carry

    lax.fori_loop(0, n_tiles, query_tile, 0)

    for d in (1, 3, 2):
        spread(d).wait_recv()
    for q, (lo, hi) in enumerate(((0, 64), (64, 112), (112, 160), (160, 224))):
        d = lax.rem(z - q + 4, 4)
        value = final[0:hi - lo].astype(F32)
        for k in range(1, 4):
            value = jnp.where(d == k, from_z[k - 1, 0:hi - lo, :].astype(F32), value)
        dk_ref[lo:hi, :] = value

    for copy in sent:
        copy.wait_send()
    for t in (n_tiles - 2, n_tiles - 1):
        dq_out(t).wait()

    def drain(g, carry):
        to_mate(4 * lax.rem(g, 2), g // 2).wait_send()
        for side in range(2):
            z_half(side, g).wait_send()
            z_whole(side, g).wait_send()
        return carry

    lax.fori_loop(0, 4, drain, 0)
    for side in range(2):
        x_half(side, 4 + x).wait_send()
        x_whole(side, 4 + x).wait_send()
    for d in (1, 2, 3):
        second_x(d).wait_send()
        second_z(d).wait_send()
        spread(d).wait_send()
        across_y(d - 1).wait_send()


def hand_on_kernel(dq_ref, dk_ref, dq_out, dk_out):
    dq_out[...] = dq_ref[...]
    dk_out[...] = dk_ref[...]


def per_device(block_order, queries, keys, dout):
    shard, heads, width = queries.shape
    rows = shard * heads
    seq = shard * lax.axis_size("ctx")
    tile, chunk, win = 256, 2 * shard, 64
    any_spec = pl.BlockSpec(memory_space=pl.ANY)
    dma = pltpu.SemaphoreType.DMA

    def half_type(*lead):
        return pltpu.VMEM((*lead, width), BF16)

    grad_queries, key_result = pl.pallas_call(
        functools.partial(attention_kernel, (shard, rows, tile, chunk, win)),
        out_shape=(jax.ShapeDtypeStruct((rows, width), BF16), jax.ShapeDtypeStruct((shard, width), F32)),
        in_specs=[pl.BlockSpec(memory_space=pltpu.SMEM), any_spec, any_spec, any_spec],
        out_specs=[any_spec, pl.BlockSpec(memory_space=pltpu.VMEM)],
        scratch_shapes=[
            half_type(seq), half_type(rows),
            pltpu.VMEM((rows, LAT), BF16),
            pltpu.VMEM((2, seq, tile), F32),
            pltpu.VMEM((seq, tile), F32),
            pltpu.VMEM((seq, rows), BF16),
            pltpu.VMEM((seq, rows), BF16),
            half_type(2, tile),
            pltpu.VMEM((2, shard, width), F32),
            half_type(4, shard), half_type(4, shard), half_type(8, shard),
            half_type(2, shard // 2), half_type(2, shard),
            half_type(2, 4, win // 2), half_type(2, 4, win), half_type(2, 4, win),
            half_type(4, win), half_type(shard), half_type(3, win), half_type(3, win),
            half_type(2, win), half_type(3, win), half_type(win), half_type(3, win),
            dma((3,)), dma((61,)), dma((61,)), dma((rows // tile,)),
            dma((4,)), dma((4,)), dma((2,)), dma((2,)), dma((2,)), dma((2,)),
            dma((2, 4)), dma((2, 4)), dma((2, 4)), dma((2, 4)),
            dma((3,)), dma((3,)), dma((3,)), dma((3,)), dma((3,)), dma((3,)), dma((3,)), dma((3,)),
        ],
        compiler_params=pltpu.CompilerParams(collective_id=0, has_side_effects=True, vmem_limit_bytes=63 << 20),
    )(block_order, keys, queries.reshape(rows, width), dout.reshape(rows, LAT))
    blocks = [pl.BlockSpec((rows // PIECES, width), lambda n: (n, 0)), pl.BlockSpec((shard // PIECES, width), lambda n: (n, 0))]
    grad_queries, key_result = pl.pallas_call(
        hand_on_kernel,
        grid=(PIECES,),
        out_shape=(jax.ShapeDtypeStruct((rows, width), BF16), jax.ShapeDtypeStruct((shard, width), F32)),
        in_specs=blocks,
        out_specs=blocks,
    )(grad_queries, key_result)
    return grad_queries.reshape(shard, heads, width), key_result


def solution(mesh):
    placed = (P(), P("ctx", "head", None), P("ctx", None), P("ctx", "head", None))
    return jax.shard_map(
        per_device,
        mesh=mesh,
        in_specs=placed,
        out_specs=(P("ctx", "head", None), P("ctx", None)),
        check_vma=False,
    )
```
